32 devices in a mesh: group: 4 (over z), shard: 8 (over y, x, core).
Axes of the slice: x: 2, y: 2, z: 4, core: 2. Of those that a mesh axis runs over, the one named last changes fastest.
Arguments:
- query_hidden: bfloat16 [32, 32, 768], P(('group', 'shard')), may hold values from -6 to 6
- positive_hidden: bfloat16 [32, 64, 768], P(('group', 'shard')), may hold values from -6 to 6
- passage_store: bfloat16 [256, 64, 768], P('shard'), may hold values from -6 to 6
- negative_ids: int32 [32, 8], P(('group', 'shard')), may hold values from 0 to 255, as said below
- teacher_margins: int32 [32, 8], P(('group', 'shard')), may hold values from -4096 to 4095
- transform_weight: bfloat16 [768, 768], replicated, may hold values from -0.21875 to 0.21875
- vocab_weight: bfloat16 [768, 15360], P(None, 'shard'), may hold values from -0.21875 to 0.21875
- dense_weight: bfloat16 [768, 768], replicated, may hold values from -0.21875 to 0.21875
Outputs:
- student_margin: float32 [32, 8], P(('group', 'shard'))
- dense_grad: float32 [768, 768], replicated
The draws below stay inside these ranges and needn't reach their ends.
Inputs may be any that keep to these rules, and one draw needn't show every extreme that they name: `negative_ids`: passage p is held by shard index p // 32. Among the 8 negatives of one index of group and shard, every store index is named by none or exactly 2 of them; one store index, drawn from the seed, is named 2 times by every index of group and shard.
All inputs are finite; a program needn't handle non-finite values.
Results may differ from the reference program's by a relative error of at most 0.0029.
Values may be sent and summed in bfloat16 or wider, within the bound.
A program may use at most 128 MiB of HBM per device.

```python
import math
import jax
import jax.numpy as jnp
from jax import lax

D = 768
LQ = 32
LP = 64
NEG = 8
CAP = 2
TRI_DEV = 1
STORE_DEV = 32
VOCAB = 15360
QUERIES = 32
PASSAGES = 256


def draw_negative_ids(key, part):
    owners = PASSAGES // STORE_DEV
    per_device = TRI_DEV * NEG
    blocks = QUERIES // TRI_DEV
    picked_count = per_device // CAP
    keys = jax.random.split(jax.random.fold_in(key, 31), 5)
    heat = jax.random.randint(keys[0], (owners,), 0, 4)
    heat = heat * heat * 256
    hottest = jax.random.randint(keys[1], (), 0, owners)
    heat = jnp.where(jnp.arange(owners) == hottest, 1 << 20, heat)
    noise = jax.random.randint(keys[2], (blocks, owners), 0, 1024)
    block_index = jnp.arange(blocks)[:, None]
    owner_index = jnp.arange(owners)[None, :]
    first_boost = (block_index == 0) & (owner_index == owners - 1)
    last_boost = (block_index == blocks - 1) & (owner_index == 0)
    boost = jnp.where(first_boost | last_boost, 1 << 19, 0)
    scores = (noise + boost + heat[None, :]) * owners + owner_index
    picked = lax.top_k(scores, picked_count)[1]
    owner_slots = jnp.repeat(picked, CAP, axis=1, total_repeat_length=per_device)
    order_key = jax.random.randint(keys[3], (blocks, per_device), 0, 4096) * per_device + jnp.arange(per_device)[None, :]
    order = jnp.argsort(order_key, axis=1, stable=True)
    owner_slots = jnp.take_along_axis(owner_slots, order, axis=1)
    local_rows = jax.random.randint(keys[4], (blocks, per_device), 0, STORE_DEV)
    local_rows = jnp.where((block_index == 0) & (owner_slots == owners - 1), STORE_DEV - 1, local_rows)
    local_rows = jnp.where((block_index == blocks - 1) & (owner_slots == 0), 0, local_rows)
    return (owner_slots * STORE_DEV + local_rows).reshape(QUERIES, NEG).astype(jnp.int32)


def set_ends(entries, stream_key, low, top_value):
    spot = [jax.random.randint(jax.random.fold_in(stream_key, axis), (), 0, length) for axis, length in enumerate(entries.shape)]
    widest = entries.shape.index(max(entries.shape))
    neighbour = spot[:widest] + [(spot[widest] + 1) % entries.shape[widest]] + spot[widest + 1:]
    return entries.at[tuple(spot)].set(low).at[tuple(neighbour)].set(top_value)


def block_scale(own_key, shape, pieces, smallest, high):
    def one(position, shards_of):
        draws = jax.random.uniform(jax.random.fold_in(jax.random.fold_in(own_key, 6), position), (shards_of,), jnp.float32, smallest / len(pieces), high / len(pieces))
        return jnp.repeat(jnp.exp(draws), shape[position] // shards_of).reshape((-1,) + (1,) * (len(shape) - position - 1))

    loudness = one(*pieces[0])
    for cut in pieces[1:]:
        loudness = loudness * one(*cut)
    return loudness


def normal_values(key, extent, scale, bound, pieces=(), kind=jnp.bfloat16):
    gain = block_scale(key, extent, pieces, -0.22, 0.18) if pieces else 1.0
    values = jax.random.normal(key, extent, jnp.float32) * scale * gain
    return jnp.minimum(jnp.maximum(values, -bound), bound).astype(kind)


def setup_inputs(seed: int = 0) -> dict:
    key_list = jax.random.split(jax.random.key(seed), 9)
    query_hidden = normal_values(key_list[0], (QUERIES, LQ, D), 1.0, 6.0, ((0, 32),))
    positive_hidden = normal_values(key_list[1], (QUERIES, LP, D), 1.0, 6.0, ((0, 32),))
    passage_store = normal_values(key_list[2], (PASSAGES, LP, D), 1.0, 6.0, ((0, 8),))
    negative_ids = draw_negative_ids(jax.random.fold_in(key_list[8], 71), 0)
    teacher_margins = set_ends(jax.random.randint(key_list[4], (QUERIES, NEG), -4096, 4096), jax.random.fold_in(key_list[4], 1), -4096, 4095).astype(jnp.int32)
    transform_weight = normal_values(key_list[5], (D, D), D ** -0.5, 0.21875)
    vocab_weight = normal_values(key_list[6], (D, VOCAB), D ** -0.5, 0.21875, ((1, 8),))
    dense_weight = normal_values(key_list[7], (D, D), D ** -0.5, 0.21875)
    return dict(query_hidden=query_hidden, positive_hidden=positive_hidden, passage_store=passage_store, negative_ids=negative_ids, teacher_margins=teacher_margins, transform_weight=transform_weight, vocab_weight=vocab_weight, dense_weight=dense_weight)


def encode(hidden, transform_weight):
    mixed_rows = jnp.dot(hidden, transform_weight, preferred_element_type=jnp.float32)
    active = jax.nn.gelu(mixed_rows, approximate=False)
    centre = lax.optimization_barrier(jnp.mean(active, axis=-1, keepdims=True))
    spread = lax.optimization_barrier(jnp.mean(jnp.square(active - centre), axis=-1, keepdims=True))
    return ((active - centre) * lax.rsqrt(spread + 1e-05)).astype(jnp.bfloat16)

def pool_rows(coded, vocab_weight):
    logits = jnp.dot(coded, vocab_weight, preferred_element_type=jnp.float32)
    return lax.optimization_barrier(jnp.max(jnp.log1p(jnp.maximum(logits, 0.0)), axis=-2))

def reference(query_hidden, positive_hidden, passage_store, negative_ids, teacher_margins, transform_weight, vocab_weight, dense_weight):
    negative_hidden = passage_store[negative_ids]
    passages = jnp.concatenate([positive_hidden[:, None], negative_hidden], axis=1)

    def one_query(pair):
        query_seq, passage_seqs = pair
        query_pool = pool_rows(encode(query_seq, transform_weight), vocab_weight)
        passage_pool = pool_rows(encode(passage_seqs, transform_weight), vocab_weight)
        return jnp.dot(passage_pool, query_pool, precision=lax.Precision.HIGHEST)
    sparse = lax.map(one_query, (query_hidden, passages)) / math.sqrt(VOCAB)
    inv_root = 1.0 / math.sqrt(D)
    query_cls = query_hidden[:, 0, :]
    positive_cls = positive_hidden[:, 0, :]
    negative_cls = negative_hidden[:, :, 0, :]
    query_vec = jnp.dot(query_cls, dense_weight, preferred_element_type=jnp.float32)
    positive_vec = jnp.dot(positive_cls, dense_weight, preferred_element_type=jnp.float32)
    negative_vec = jnp.dot(negative_cls, dense_weight, preferred_element_type=jnp.float32)
    dense_pos = lax.optimization_barrier(jnp.sum(query_vec * positive_vec, axis=1)) * inv_root
    dense_neg = jnp.einsum('qd,qkd->qk', query_vec, negative_vec, precision=lax.Precision.HIGHEST) * inv_root
    pos_score = sparse[:, 0] + dense_pos
    neg_score = sparse[:, 1:] + dense_neg
    margin = pos_score[:, None] - neg_score
    target = teacher_margins.astype(jnp.float32) / 1024.0
    coef = (margin - target) / NEG
    coef_total = lax.optimization_barrier(jnp.sum(coef, axis=1))
    grad_query = (coef_total[:, None] * positive_vec - jnp.einsum('qk,qkd->qd', coef, negative_vec, precision=lax.Precision.HIGHEST)) * inv_root
    grad_positive = coef_total[:, None] * query_vec * inv_root
    grad_negative = -coef[:, :, None] * query_vec[:, None, :] * inv_root
    states = jnp.concatenate([query_cls, positive_cls, negative_cls.reshape(-1, D)], axis=0).astype(jnp.float32)
    factors = jnp.concatenate([grad_query, grad_positive, grad_negative.reshape(-1, D)], axis=0)
    dense_grad = jnp.einsum('rd,re->de', states, factors, precision=lax.Precision.HIGHEST)
    return (margin, dense_grad)
```

```python
import functools
import math

import jax
import jax.numpy as jnp
from jax import lax
from jax.experimental import pallas as pl
from jax.experimental.pallas import tpu as pltpu
from jax.sharding import PartitionSpec as P

COLS = 640
LANES = 128
AHEAD = 2
MESH_ID = pl.DeviceIdType.MESH


def encode(hidden, transform_weight):
    mixed = jnp.dot(hidden, transform_weight, preferred_element_type=jnp.float32)
    active = 0.5 * mixed * (1.0 + lax.erf(mixed * math.sqrt(0.5)))
    centre = jnp.mean(active, axis=-1, keepdims=True)
    shifted = active - centre
    spread = jnp.mean(shifted * shifted, axis=-1, keepdims=True)
    return (shifted * lax.rsqrt(spread + 1e-05)).astype(jnp.bfloat16)


def chunk_sizes(share):
    sizes = []
    while share > 1:
        sizes.append(2)
        share -= 2
    return sizes + [1] * share


def halves(values):
    high = values.astype(jnp.bfloat16)
    return high, (values - high.astype(jnp.float32)).astype(jnp.bfloat16)


def exchange_kernel(
    groups,
    shards,
    vocab_total,
    sizes,
    ids_ref,
    teacher_ref,
    query_hbm,
    positive_hbm,
    transform_hbm,
    store_hbm,
    vocab_hbm,
    dense_hbm,
    left_out,
    right_out,
    margin_out,
    query,
    positive,
    transform,
    hidden,
    vocab,
    dense,
    labels_buf,
    front,
    coded,
    cls_all,
    query_pool,
    positive_pool,
    pool_buf,
    states,
    vectors,
    places,
    early,
    dense_margin,
    partial,
    tables,
    margin_buf,
    load_sem,
    tree_send,
    tree_recv,
    z_send,
    z_recv,
    sum_send,
    sum_recv,
):
    group = lax.axis_index("group")
    shard = lax.axis_index("shard")
    devices = groups * shards
    linear = group * shards + shard
    bits = shards.bit_length() - 1
    queries, lq, width = query.shape
    share, lp, _ = hidden.shape
    columns = vocab.shape[1]
    negatives = ids_ref.shape[1]
    store_rows = share * groups
    cls_rows = cls_all.shape[3]
    total = devices * queries
    plane = shards * queries
    half_slots = shards // 2
    block_rows = pool_buf.shape[2]
    firsts = [sum(sizes[:c]) for c in range(len(sizes))]
    count = len(sizes) + 1
    positive_rows = queries * lp
    query_rows = queries * lq

    digit = [(shard // (1 << i)) % 2 for i in range(bits)]

    def partner(offset):
        index = 0
        for i in range(bits):
            index = index + ((1 - digit[i]) if (offset >> i) & 1 else digit[i]) * (1 << i)
        return index

    peers = [partner(offset) for offset in range(shards)]

    barrier = pltpu.get_barrier_semaphore()
    for offset in range(1, shards):
        pl.semaphore_signal(
            barrier, inc=1, device_id={"shard": peers[offset]}, device_id_type=MESH_ID
        )
    for i in range(1, groups):
        pl.semaphore_signal(
            barrier, inc=1, device_id={"group": (group + i) % groups}, device_id_type=MESH_ID
        )

    pairs = (
        (transform_hbm, transform),
        (query_hbm, query),
        (positive_hbm, positive),
        (store_hbm.at[pl.ds(group * share, share)], hidden),
        (vocab_hbm, vocab),
        (dense_hbm, dense),
    )
    loads = [
        pltpu.make_async_copy(source, target, load_sem.at[i])
        for i, (source, target) in enumerate(pairs)
    ]
    for load in loads:
        load.start()

    def block(chunk, slot, piece):
        if chunk == 0:
            start, rows = 0, front.shape[1]
        else:
            start, rows = firsts[chunk - 1] * lp, sizes[chunk - 1] * lp
        middle = (rows // 2 + 15) // 16 * 16
        if piece == 1:
            start, rows = start, middle
        elif piece == 2:
            start, rows = start + middle, rows - middle
        ref = front if chunk == 0 else coded
        return ref.at[slot, pl.ds(start, rows)]

    def order(piece):
        outer = list(range(1, bits))
        return outer if piece == 1 else outer[::-1]

    def channel(offset):
        if offset % 2 == 0:
            return offset // 2 - 1
        return half_slots - 1 + offset // half_slots

    def hop(chunk, offset, piece, dim):
        ref = block(chunk, peers[offset], piece)
        return pltpu.make_async_remote_copy(
            src_ref=ref,
            dst_ref=ref,
            send_sem=tree_send.at[min(chunk, 1)],
            recv_sem=tree_recv.at[chunk, channel(offset ^ (1 << dim))],
            device_id={"shard": peers[1 << dim]},
            device_id_type=MESH_ID,
        )

    def send(*key):
        hop(*key).start()

    def send_own(chunk):
        for dim in list(range(1, bits)) + [0]:
            send(chunk, 0, 0, dim)

    def whole(chunk, slots):
        if chunk == 0:
            return front.at[:slots]
        rows = sizes[chunk - 1] * lp
        return coded.at[:slots, pl.ds(firsts[chunk - 1] * lp, rows)]

    def arrived(chunk, place, slots):
        ref = whole(chunk, slots)
        pltpu.make_async_copy(ref, ref, tree_recv.at[chunk, place]).wait()

    def relay(chunk, level):
        for offset in range(2, shards, 2):
            if offset.bit_count() == level:
                arrived(chunk, channel(offset), 1)
                for piece in (1, 2):
                    path = order(piece)
                    last = max(path.index(i) for i in range(1, bits) if (offset >> i) & 1)
                    for dim in path[last + 1 :]:
                        send(chunk, offset, piece, dim)
                send(chunk, offset, 0, 0)

    def finish(chunk, half):
        arrived(chunk, half_slots - 1 + half, half_slots // 2)

    def first_token(values):
        values = values.astype(jnp.float32)
        token = lax.broadcasted_iota(jnp.int32, values.shape, 1)
        return jnp.sum(jnp.where(token == 0, values, 0.0), axis=1)

    def pool(rows, length):
        parts = []
        sequences = rows.shape[0] // length
        for start in range(0, columns, COLS):
            stop = min(start + COLS, columns)
            logits = jnp.dot(rows, vocab[:, start:stop], preferred_element_type=jnp.float32)
            best = jnp.max(logits.reshape(sequences, length, stop - start), axis=1)
            parts.append((start, stop, jnp.log1p(jnp.maximum(best, 0.0))))
        return parts

    def pool_front():
        rows = front[:, positive_rows : positive_rows + query_rows]
        for start, stop, values in pool(rows.reshape(plane * lq, width), lq):
            high = values.astype(jnp.bfloat16).astype(jnp.float32)
            both = jnp.concatenate([high, values - high], axis=0)
            query_pool[group, :, start:stop] = both.astype(jnp.bfloat16)
        for i in range(1, groups):
            z_copy(i, 1).start()
        rows = front[:, :positive_rows].reshape(plane * lp, width)
        for start, stop, values in pool(rows, lp):
            positive_pool[:, start:stop] = values

    top = shard // half_slots

    def pool_half(chunk, half):
        side = top if half == 0 else 1 - top
        start, size = firsts[chunk - 1] * lp, sizes[chunk - 1]
        rows = coded[pl.ds(side * half_slots, half_slots), start : start + size * lp]
        tall = half_slots * size
        for first, last, values in pool(rows.reshape(tall * lp, width), lp):
            pool_buf[chunk - 1, side, :tall, first:last] = values

    parity = shard % 2

    def z_part(kind, slot):
        return query_pool.at[slot] if kind else cls_all.at[slot, parity]

    def z_copy(i, kind):
        return pltpu.make_async_remote_copy(
            src_ref=z_part(kind, group),
            dst_ref=z_part(kind, group),
            send_sem=z_send.at[kind],
            recv_sem=z_recv.at[kind],
            device_id={"group": (group + i) % groups},
            device_id_type=MESH_ID,
        )

    def others(kind):
        if kind == 1:
            return query_pool.at[: groups - 1]
        return cls_all.at[: groups - 1, 0]

    def wait_bytes(ref, sem):
        pltpu.make_async_copy(ref, ref, sem).wait()

    def z_pass():
        wait_bytes(others(0), z_recv.at[0])
        for i in range(1, groups):
            slot = (group + i) % groups
            pltpu.make_async_remote_copy(
                src_ref=cls_all.at[slot, parity],
                dst_ref=cls_all.at[slot, parity],
                send_sem=z_send.at[2],
                recv_sem=z_recv.at[2],
                device_id={"shard": peers[1]},
                device_id_type=MESH_ID,
            ).start()

    def dense_work():
        wait_bytes(others(0), z_recv.at[2])
        table = cls_all[...].reshape(devices * cls_rows, width)
        spots = devices * cls_rows
        spot = lax.broadcasted_iota(jnp.int32, (total, spots), 1)
        row = lax.broadcasted_iota(jnp.int32, (total, spots), 0)
        def column_of(g, s):
            return ((g * 2 + s % 2) * half_slots + s // 2) * cls_rows

        device = row // queries
        base = column_of(device // shards, device % shards) + share + row % queries

        def pick(wanted, values):
            chosen = jnp.where(spot == wanted, 1.0, 0.0).astype(jnp.bfloat16)
            return jnp.dot(chosen, values, preferred_element_type=jnp.float32)

        labels = pick(base + 2 * queries, table[:, :LANES])
        states[0] = pick(base, table)
        states[1] = pick(base + queries, table)
        lane = lax.broadcasted_iota(jnp.int32, (total, LANES), 1)
        for k in range(negatives):
            number = (labels[:, k : k + 1] * 256.0 + labels[:, negatives + k : negatives + k + 1])
            number = number.astype(jnp.int32)
            owner = number // store_rows
            local = number - owner * store_rows
            part = local // share
            inner = local - part * share
            states[2 + k] = pick(column_of(part, owner) + inner, table)
            side = owner // half_slots
            slot = owner - side * half_slots
            place = jnp.zeros_like(number)
            for c, (size, first) in enumerate(zip(sizes, firsts, strict=True)):
                spot_here = (2 * c + side) * block_rows + slot * size + inner - first
                place = jnp.where((inner >= first) & (inner < first + size), spot_here, place)
            place = jnp.where(part == group, place, -1)
            places[k] = jnp.broadcast_to(place, (total, LANES))
        flat = states[...].reshape((2 + negatives) * total, width).astype(jnp.bfloat16)
        vectors[...] = jnp.dot(flat, dense[...], preferred_element_type=jnp.float32).reshape(
            vectors.shape
        )
        inv_root = 1.0 / math.sqrt(width)
        query_vec = vectors[0]
        dense_pos = jnp.sum(query_vec * vectors[1], axis=1, keepdims=True)
        result = jnp.zeros((total, LANES), jnp.float32)
        for k in range(negatives):
            dense_neg = jnp.sum(query_vec * vectors[2 + k], axis=1, keepdims=True)
            target = (
                labels[:, 2 * negatives + k : 2 * negatives + k + 1] * 64.0
                + labels[:, 3 * negatives + k : 3 * negatives + k + 1]
            ) / 1024.0
            result = jnp.where(lane == k, (dense_pos - dense_neg) * inv_root, result)
            result = jnp.where(lane == negatives + k, target, result)
        dense_margin[...] = result
        query_bf = states[0].astype(jnp.bfloat16)
        query_high, query_low = halves(query_vec)
        left_out[:total] = query_bf
        left_out[total : 2 * total] = query_bf
        right_out[2 * total : 3 * total] = query_high
        right_out[3 * total : 4 * total] = query_high
        right_out[4 * total : 5 * total] = query_low

    def score(values):
        high, low = halves(values)
        stacked = query_pool[...].reshape(2 * total, columns)
        dims = (((1,), (1,)), ((), ()))
        both = lax.dot_general(
            stacked, high, dims, preferred_element_type=jnp.float32
        ) + lax.dot_general(stacked, low, dims, preferred_element_type=jnp.float32)
        both = both.reshape(groups, 2, plane, values.shape[0])
        return (both[:, 0] + both[:, 1]).reshape(total, values.shape[0])

    lane = lax.broadcasted_iota(jnp.int32, (total, LANES), 1)

    def pick_scores(first, last):
        rows = (last - first) * 2 * block_rows
        values = score(pool_buf[first:last].reshape(rows, columns))
        column = lax.broadcasted_iota(jnp.int32, values.shape, 1) + first * 2 * block_rows
        result = jnp.zeros((total, LANES), jnp.float32)
        for k in range(negatives):
            hit = column == places[k, :, :rows]
            taken = jnp.sum(jnp.where(hit, values, 0.0), axis=1, keepdims=True)
            result = jnp.where(lane == k, taken, result)
        return result

    def early_scores():
        wait_bytes(others(1), z_recv.at[1])
        values = score(positive_pool[...])
        row = lax.broadcasted_iota(jnp.int32, values.shape, 0)
        column = lax.broadcasted_iota(jnp.int32, values.shape, 1)
        own = jnp.sum(
            jnp.where(row == group * plane + column, values, 0.0), axis=1, keepdims=True
        )
        result = jnp.where(lane < negatives, own, 0.0)
        if count > 2:
            result = result - pick_scores(0, count - 2)
        early[...] = result

    for load in loads[:3]:
        load.wait()
    rows = jnp.concatenate(
        [
            positive[...].reshape(positive_rows, width),
            query[...].reshape(query_rows, width),
        ],
        axis=0,
    )
    front[shard, : positive_rows + query_rows] = encode(rows, transform[...])
    loads[3].wait()
    labels_buf[...] = jnp.zeros_like(labels_buf)
    labels_buf[:share] = first_token(hidden[:, :16])
    labels_buf[share : share + queries] = first_token(query[:, :16])
    labels_buf[share + queries : share + 2 * queries] = first_token(positive[:, :16])
    numbers, marks = ids_ref[...], teacher_ref[...]
    upper = numbers // 256
    level = (marks + 4096) // 64
    for i, values in enumerate((upper, numbers - upper * 256, level - 64, marks + 4096 - level * 64)):
        labels_buf[
            share + 2 * queries : share + 3 * queries, i * negatives : (i + 1) * negatives
        ] = values.astype(jnp.float32)
    front[shard, positive_rows + query_rows :] = labels_buf[...].astype(jnp.bfloat16)
    pl.semaphore_wait(barrier, shards + groups - 2)

    send_own(0)
    for chunk in range(1, count):
        first, size = firsts[chunk - 1], sizes[chunk - 1]
        rows = hidden[first : first + size].reshape(size * lp, width)
        coded[shard, first * lp : (first + size) * lp] = encode(rows, transform[...])
        if chunk < AHEAD:
            send_own(chunk)
    pool_buf[...] = jnp.zeros_like(pool_buf)
    loads[4].wait()
    loads[5].wait()

    for step in range(count + bits - 2):
        ahead = step + AHEAD
        for level in range(1, bits):
            chunk = step - level + 1
            if 0 <= chunk < count:
                relay(chunk, level)
                if level == 1 and ahead < count:
                    send_own(ahead)
                if level == bits - 2:
                    finish(chunk, 0)
                    if chunk > 0:
                        pool_half(chunk, 0)
                if level == bits - 1:
                    finish(chunk, 1)
                    if chunk == 0:
                        for slot in range(shards):
                            cls_all[group, slot % 2, slot // 2] = front[
                                slot, positive_rows + query_rows :
                            ]
                        for i in range(1, groups):
                            z_copy(i, 0).start()
                        pool_front()
                    else:
                        pool_half(chunk, 1)
                    if chunk == max(1, count - 3):
                        z_pass()
                    if chunk == max(1, count - 2):
                        dense_work()
        if step == count + bits - 4:
            early_scores()

    partial[shard] = early[...] - pick_scores(count - 2, count - 1)

    for offset in range(shards - 1, 0, -1):
        pltpu.make_async_remote_copy(
            src_ref=partial.at[shard],
            dst_ref=partial.at[shard],
            send_sem=sum_send.at[0],
            recv_sem=sum_recv.at[0],
            device_id={"shard": peers[offset]},
            device_id_type=MESH_ID,
        ).start()
    wait_bytes(front.at[: shards - 1], tree_send.at[0])
    wait_bytes(coded.at[: shards - 1], tree_send.at[1])
    wait_bytes(others(0), z_send.at[0])
    wait_bytes(others(1), z_send.at[1])
    wait_bytes(others(0), z_send.at[2])
    wait_bytes(partial.at[: shards - 1], sum_recv.at[0])
    tables[group] = jnp.sum(partial[...], axis=0)
    for i in range(groups - 1, 0, -1):
        pltpu.make_async_remote_copy(
            src_ref=tables.at[group],
            dst_ref=tables.at[group],
            send_sem=sum_send.at[1],
            recv_sem=sum_recv.at[1],
            device_id={"group": (group + i) % groups},
            device_id_type=MESH_ID,
        ).start()
    wait_bytes(partial.at[: shards - 1], sum_send.at[0])
    wait_bytes(tables.at[: groups - 1], sum_recv.at[1])

    other = dense_margin[...]
    margin = jnp.sum(tables[...], axis=0) * (1.0 / math.sqrt(vocab_total)) + other
    margin_buf[...] = margin
    margin_out[...] = margin_buf[pl.ds(linear * queries, queries), :negatives]
    scale = 1.0 / (negatives * math.sqrt(width))
    coefs = [
        (margin[:, k : k + 1] - other[:, negatives + k : negatives + k + 1]) * scale
        for k in range(negatives)
    ]
    together = sum(coefs[1:], coefs[0])
    ahead_vec = together * vectors[1]
    ahead_cls = together * states[1]
    for k in range(negatives):
        ahead_vec = ahead_vec - coefs[k] * vectors[2 + k]
        ahead_cls = ahead_cls - coefs[k] * states[2 + k]
    high, low = halves(ahead_vec)
    right_out[:total] = high
    right_out[total : 2 * total] = low
    high, low = halves(ahead_cls)
    left_out[2 * total : 3 * total] = high
    left_out[3 * total : 4 * total] = low
    left_out[4 * total :] = high
    wait_bytes(tables.at[: groups - 1], sum_send.at[1])


def gradient_kernel(
    left_hbm, right_hbm, margin_hbm, margin_out, grad_ref, left, right, margin, load_sem
):
    pairs = ((left_hbm, left), (right_hbm, right), (margin_hbm, margin))
    loads = [
        pltpu.make_async_copy(source, target, load_sem.at[i])
        for i, (source, target) in enumerate(pairs)
    ]
    for load in loads:
        load.start()
    for load in loads:
        load.wait()
    margin_out[...] = margin[...]
    grad_ref[...] = lax.dot_general(
        left[...],
        right[...],
        (((0,), (0,)), ((), ())),
        preferred_element_type=jnp.float32,
    )


def body(
    query_hidden,
    positive_hidden,
    passage_store,
    negative_ids,
    teacher_margins,
    transform_weight,
    vocab_weight,
    dense_weight,
):
    groups = lax.axis_size("group")
    shards = lax.axis_size("shard")
    devices = groups * shards
    bits = shards.bit_length() - 1
    queries, lq, width = query_hidden.shape
    store_rows, lp, _ = passage_store.shape
    negatives = negative_ids.shape[1]
    columns = vocab_weight.shape[1]
    share = store_rows // groups
    sizes = chunk_sizes(share)
    count = len(sizes) + 1
    cls_rows = share + 3 * queries
    cls_rows += -cls_rows % 16
    total = devices * queries
    plane = shards * queries
    block_rows = shards // 2 * max(sizes)
    block_rows += -block_rows % 8

    vmem = pl.BlockSpec(memory_space=pltpu.VMEM)
    hbm = pl.BlockSpec(memory_space=pl.ANY)
    dma = pltpu.SemaphoreType.DMA
    bf16, f32 = jnp.bfloat16, jnp.float32
    left, right, margin = pl.pallas_call(
        functools.partial(exchange_kernel, groups, shards, columns * shards, sizes),
        out_shape=[
            jax.ShapeDtypeStruct((5 * total, width), bf16),
            jax.ShapeDtypeStruct((5 * total, width), bf16),
            jax.ShapeDtypeStruct((queries, negatives), f32),
        ],
        in_specs=[vmem] * 2 + [hbm] * 6,
        out_specs=[vmem] * 3,
        scratch_shapes=[
            pltpu.VMEM((queries, lq, width), bf16),
            pltpu.VMEM((queries, lp, width), bf16),
            pltpu.VMEM((width, width), bf16),
            pltpu.VMEM((share, lp, width), bf16),
            pltpu.VMEM((width, columns), bf16),
            pltpu.VMEM((width, width), bf16),
            pltpu.VMEM((cls_rows, width), f32),
            pltpu.VMEM((shards, queries * (lq + lp) + cls_rows, width), bf16),
            pltpu.VMEM((shards, share * lp, width), bf16),
            pltpu.VMEM((groups, 2, shards // 2, cls_rows, width), bf16),
            pltpu.VMEM((groups, 2 * plane, columns), bf16),
            pltpu.VMEM((plane, columns), f32),
            pltpu.VMEM((len(sizes), 2, block_rows, columns), f32),
            pltpu.VMEM((2 + negatives, total, width), f32),
            pltpu.VMEM((2 + negatives, total, width), f32),
            pltpu.VMEM((negatives, total, LANES), jnp.int32),
            pltpu.VMEM((total, LANES), f32),
            pltpu.VMEM((total, LANES), f32),
            pltpu.VMEM((shards, total, LANES), f32),
            pltpu.VMEM((groups, total, LANES), f32),
            pltpu.VMEM((total, LANES), f32),
            dma((6,)),
            dma((2,)),
            dma((count, shards // 2 + 1)),
            dma((3,)),
            dma((3,)),
            dma((2,)),
            dma((2,)),
        ],
        compiler_params=pltpu.CompilerParams(
            collective_id=0, has_side_effects=True, vmem_limit_bytes=58 * 1024 * 1024
        ),
        name="exchange",
    )(
        negative_ids,
        teacher_margins,
        query_hidden,
        positive_hidden,
        transform_weight,
        passage_store,
        vocab_weight,
        dense_weight,
    )
    return pl.pallas_call(
        gradient_kernel,
        out_shape=[
            jax.ShapeDtypeStruct((queries, negatives), f32),
            jax.ShapeDtypeStruct((width, width), f32),
        ],
        in_specs=[hbm] * 3,
        out_specs=[vmem] * 2,
        scratch_shapes=[
            pltpu.VMEM((5 * total, width), bf16),
            pltpu.VMEM((5 * total, width), bf16),
            pltpu.VMEM((queries, negatives), f32),
            dma((3,)),
        ],
        compiler_params=pltpu.CompilerParams(vmem_limit_bytes=58 * 1024 * 1024),
        name="gradient",
    )(left, right, margin)


def solution(mesh):
    in_specs = (
        P(("group", "shard"), None, None),
        P(("group", "shard"), None, None),
        P("shard", None, None),
        P(("group", "shard"), None),
        P(("group", "shard"), None),
        P(),
        P(None, "shard"),
        P(),
    )
    out_specs = (P(("group", "shard"), None), P())
    return jax.shard_map(body, mesh=mesh, in_specs=in_specs, out_specs=out_specs, check_vma=False)
```

```python
import functools
import math

import jax
import jax.numpy as jnp
from jax import lax
from jax.experimental import pallas as pl
from jax.experimental.pallas import tpu as pltpu
from jax.sharding import PartitionSpec as P

COLS = 640
LANES = 128
MESH_ID = pl.DeviceIdType.MESH


def encode(hidden, transform_weight):
    mixed = jnp.dot(hidden, transform_weight, preferred_element_type=jnp.float32)
    active = 0.5 * mixed * (1.0 + lax.erf(mixed * math.sqrt(0.5)))
    centre = jnp.mean(active, axis=-1, keepdims=True)
    shifted = active - centre
    spread = jnp.mean(shifted * shifted, axis=-1, keepdims=True)
    return (shifted * lax.rsqrt(spread + 1e-05)).astype(jnp.bfloat16)


def chunk_sizes(share):
    sizes = []
    while share > 1:
        sizes.append(2)
        share -= 2
    return sizes + [1] * share


def halves(values):
    high = values.astype(jnp.bfloat16)
    return high, (values - high.astype(jnp.float32)).astype(jnp.bfloat16)


def exchange_kernel(
    groups,
    shards,
    vocab_total,
    sizes,
    ids_ref,
    teacher_ref,
    query_hbm,
    positive_hbm,
    transform_hbm,
    store_hbm,
    vocab_hbm,
    dense_hbm,
    left_out,
    right_out,
    margin_out,
    query,
    positive,
    transform,
    hidden,
    vocab,
    dense,
    labels_buf,
    front,
    coded,
    cls_all,
    query_pool,
    positive_pool,
    pool_buf,
    states,
    vectors,
    places,
    early,
    dense_margin,
    partial,
    tables,
    margin_buf,
    load_sem,
    tree_send,
    tree_recv,
    z_send,
    z_recv,
    sum_send,
    sum_recv,
):
    group = lax.axis_index("group")
    shard = lax.axis_index("shard")
    devices = groups * shards
    linear = group * shards + shard
    bits = shards.bit_length() - 1
    queries, lq, width = query.shape
    share, lp, _ = hidden.shape
    columns = vocab.shape[1]
    negatives = ids_ref.shape[1]
    store_rows = share * groups
    cls_rows = cls_all.shape[3]
    total = devices * queries
    plane = shards * queries
    half_slots = shards // 2
    quarter = shards // 4
    parity = shard % 2
    top = shard // half_slots
    block_rows = pool_buf.shape[2]
    firsts = [sum(sizes[:c]) for c in range(len(sizes))]
    count = len(sizes) + 1
    positive_rows = queries * lp
    query_rows = queries * lq

    digit = [(shard // (1 << i)) % 2 for i in range(bits)]

    def partner(offset):
        index = 0
        for i in range(bits):
            index = index + ((1 - digit[i]) if (offset >> i) & 1 else digit[i]) * (1 << i)
        return index

    peers = [partner(offset) for offset in range(shards)]

    barrier = pltpu.get_barrier_semaphore()
    for offset in range(1, shards):
        pl.semaphore_signal(
            barrier, inc=1, device_id={"shard": peers[offset]}, device_id_type=MESH_ID
        )
    for i in range(1, groups):
        pl.semaphore_signal(
            barrier, inc=1, device_id={"group": (group + i) % groups}, device_id_type=MESH_ID
        )

    pairs = (
        (transform_hbm, transform),
        (query_hbm, query),
        (positive_hbm, positive),
        (store_hbm.at[pl.ds(group * share, share)], hidden),
        (vocab_hbm, vocab),
        (dense_hbm, dense),
    )
    loads = [
        pltpu.make_async_copy(source, target, load_sem.at[i])
        for i, (source, target) in enumerate(pairs)
    ]
    for load in loads:
        load.start()

    def block(chunk, slot, piece):
        if chunk == 0:
            start, rows = 0, front.shape[2]
        else:
            start, rows = firsts[chunk - 1] * lp, sizes[chunk - 1] * lp
        middle = (rows // 2 + 15) // 16 * 16
        if piece == 1:
            start, rows = start, middle
        elif piece == 2:
            start, rows = start + middle, rows - middle
        ref = front if chunk == 0 else coded
        return ref.at[slot % 2, slot // 2, pl.ds(start, rows)]

    def order(piece):
        outer = list(range(1, bits))
        return outer if piece == 1 else outer[::-1]

    def channel(offset):
        return offset // 2 - 1

    def hop(chunk, offset, piece, dim):
        ref = block(chunk, peers[offset], piece)
        return pltpu.make_async_remote_copy(
            src_ref=ref,
            dst_ref=ref,
            send_sem=tree_send.at[min(chunk, 1)],
            recv_sem=tree_recv.at[chunk, channel(offset ^ (1 << dim))],
            device_id={"shard": peers[1 << dim]},
            device_id_type=MESH_ID,
        )

    def send(*key):
        hop(*key).start()

    def send_own(chunk):
        for dim in range(1, bits):
            send(chunk, 0, 0, dim)

    def send_core(chunk, half):
        side = top if half == 0 else 1 - top
        place = pl.ds(side * quarter, quarter)
        if chunk == 0:
            ref = front.at[parity, place]
        else:
            rows = sizes[chunk - 1] * lp
            ref = coded.at[parity, place, pl.ds(firsts[chunk - 1] * lp, rows)]
        pltpu.make_async_remote_copy(
            src_ref=ref,
            dst_ref=ref,
            send_sem=tree_send.at[min(chunk, 1)],
            recv_sem=tree_recv.at[chunk, half_slots - 1 + half],
            device_id={"shard": peers[1]},
            device_id_type=MESH_ID,
        ).start()

    def whole(chunk, slots):
        if chunk == 0:
            return front.at[0, :slots]
        rows = sizes[chunk - 1] * lp
        return coded.at[0, :slots, pl.ds(firsts[chunk - 1] * lp, rows)]

    def arrived(chunk, place, slots):
        ref = whole(chunk, slots)
        pltpu.make_async_copy(ref, ref, tree_recv.at[chunk, place]).wait()

    def relay(chunk, level):
        for offset in range(2, shards, 2):
            if offset.bit_count() == level:
                arrived(chunk, channel(offset), 1)
                for piece in (1, 2):
                    path = order(piece)
                    last = max(path.index(i) for i in range(1, bits) if (offset >> i) & 1)
                    for dim in path[last + 1 :]:
                        send(chunk, offset, piece, dim)

    def finish(chunk, half):
        arrived(chunk, half_slots - 1 + half, quarter)

    def first_token(values):
        values = values.astype(jnp.float32)
        token = lax.broadcasted_iota(jnp.int32, values.shape, 1)
        return jnp.sum(jnp.where(token == 0, values, 0.0), axis=1)

    def pool(rows, length):
        parts = []
        sequences = rows.shape[0] // length
        for start in range(0, columns, COLS):
            stop = min(start + COLS, columns)
            logits = jnp.dot(rows, vocab[:, start:stop], preferred_element_type=jnp.float32)
            best = jnp.max(logits.reshape(sequences, length, stop - start), axis=1)
            parts.append((start, stop, jnp.log1p(jnp.maximum(best, 0.0))))
        return parts

    def pool_query():
        rows = front[:, :, positive_rows : positive_rows + query_rows]
        for start, stop, values in pool(rows.reshape(plane * lq, width), lq):
            high = values.astype(jnp.bfloat16).astype(jnp.float32)
            both = jnp.concatenate([high, values - high], axis=0)
            query_pool[group, :, start:stop] = both.astype(jnp.bfloat16)
        for i in range(1, groups):
            z_copy(i, 1).start()

    def pool_positive():
        rows = front[:, :, :positive_rows].reshape(plane * lp, width)
        for start, stop, values in pool(rows, lp):
            positive_pool[:, start:stop] = values

    def pool_half(chunk, half):
        side = top if half == 0 else 1 - top
        start, size = firsts[chunk - 1] * lp, sizes[chunk - 1]
        rows = coded[:, pl.ds(side * quarter, quarter), start : start + size * lp]
        tall = half_slots * size
        for first, last, values in pool(rows.reshape(tall * lp, width), lp):
            pool_buf[chunk - 1, side, :tall, first:last] = values

    def z_part(kind, slot):
        return query_pool.at[slot] if kind else cls_all.at[slot, parity]

    def z_copy(i, kind):
        return pltpu.make_async_remote_copy(
            src_ref=z_part(kind, group),
            dst_ref=z_part(kind, group),
            send_sem=z_send.at[kind],
            recv_sem=z_recv.at[kind],
            device_id={"group": (group + i) % groups},
            device_id_type=MESH_ID,
        )

    def others(kind):
        if kind == 1:
            return query_pool.at[: groups - 1]
        return cls_all.at[: groups - 1, 0]

    def wait_bytes(ref, sem):
        pltpu.make_async_copy(ref, ref, sem).wait()

    def z_pass():
        wait_bytes(others(0), z_recv.at[0])
        for i in range(1, groups):
            slot = (group + i) % groups
            pltpu.make_async_remote_copy(
                src_ref=cls_all.at[slot, parity],
                dst_ref=cls_all.at[slot, parity],
                send_sem=z_send.at[2],
                recv_sem=z_recv.at[2],
                device_id={"shard": peers[1]},
                device_id_type=MESH_ID,
            ).start()

    def dense_work():
        wait_bytes(others(0), z_recv.at[2])
        table = cls_all[...].reshape(devices * cls_rows, width)
        spots = devices * cls_rows
        spot = lax.broadcasted_iota(jnp.int32, (total, spots), 1)
        row = lax.broadcasted_iota(jnp.int32, (total, spots), 0)
        base = (row // queries) * cls_rows + share + row % queries

        def pick(wanted, values):
            chosen = jnp.where(spot == wanted, 1.0, 0.0).astype(jnp.bfloat16)
            return jnp.dot(chosen, values, preferred_element_type=jnp.float32)

        labels = pick(base + 2 * queries, table[:, :LANES])
        states[0] = pick(base, table)
        states[1] = pick(base + queries, table)
        lane = lax.broadcasted_iota(jnp.int32, (total, LANES), 1)
        for k in range(negatives):
            number = (labels[:, k : k + 1] * 256.0 + labels[:, negatives + k : negatives + k + 1])
            number = number.astype(jnp.int32)
            owner = number // store_rows
            local = number - owner * store_rows
            part = local // share
            inner = local - part * share
            spot_of = (part * 2 + owner % 2) * half_slots + owner // 2
            states[2 + k] = pick(spot_of * cls_rows + inner, table)
            side = owner // half_slots
            twin = owner % 2
            slot = twin * quarter + (owner - side * half_slots) // 2
            place = jnp.zeros_like(number)
            for c, (size, first) in enumerate(zip(sizes, firsts, strict=True)):
                spot_here = (2 * c + side) * block_rows + slot * size + inner - first
                place = jnp.where((inner >= first) & (inner < first + size), spot_here, place)
            place = jnp.where(part == group, place, -1)
            places[k] = jnp.broadcast_to(place, (total, LANES))
        flat = states[...].reshape((2 + negatives) * total, width).astype(jnp.bfloat16)
        vectors[...] = jnp.dot(flat, dense[...], preferred_element_type=jnp.float32).reshape(
            vectors.shape
        )
        inv_root = 1.0 / math.sqrt(width)
        query_vec = vectors[0]
        dense_pos = jnp.sum(query_vec * vectors[1], axis=1, keepdims=True)
        result = jnp.zeros((total, LANES), jnp.float32)
        for k in range(negatives):
            dense_neg = jnp.sum(query_vec * vectors[2 + k], axis=1, keepdims=True)
            target = (
                labels[:, 2 * negatives + k : 2 * negatives + k + 1] * 64.0
                + labels[:, 3 * negatives + k : 3 * negatives + k + 1]
            ) / 1024.0
            result = jnp.where(lane == k, (dense_pos - dense_neg) * inv_root, result)
            result = jnp.where(lane == negatives + k, target, result)
        dense_margin[...] = result
        query_bf = states[0].astype(jnp.bfloat16)
        query_high, query_low = halves(query_vec)
        left_out[:total] = query_bf
        left_out[total : 2 * total] = query_bf
        right_out[2 * total : 3 * total] = query_high
        right_out[3 * total : 4 * total] = query_high
        right_out[4 * total : 5 * total] = query_low

    def score(values):
        high, low = halves(values)
        stacked = query_pool[...].reshape(2 * total, columns)
        dims = (((1,), (1,)), ((), ()))
        both = lax.dot_general(
            stacked, high, dims, preferred_element_type=jnp.float32
        ) + lax.dot_general(stacked, low, dims, preferred_element_type=jnp.float32)
        both = both.reshape(groups, 2, plane, values.shape[0])
        return (both[:, 0] + both[:, 1]).reshape(total, values.shape[0])

    spread = partial.shape[2]
    lane = lax.broadcasted_iota(jnp.int32, (total, spread), 1)
    lane -= (lax.broadcasted_iota(jnp.int32, (total, spread), 0) // 8) * negatives

    def pick_scores(first, last):
        rows = (last - first) * 2 * block_rows
        values = score(pool_buf[first:last].reshape(rows, columns))
        column = lax.broadcasted_iota(jnp.int32, values.shape, 1) + first * 2 * block_rows
        result = jnp.zeros((total, spread), jnp.float32)
        for k in range(negatives):
            hit = column == places[k, :, :rows]
            taken = jnp.sum(jnp.where(hit, values, 0.0), axis=1, keepdims=True)
            result = jnp.where(lane == k, taken, result)
        return result

    def early_scores():
        wait_bytes(others(1), z_recv.at[1])
        values = score(positive_pool[...])
        row = lax.broadcasted_iota(jnp.int32, values.shape, 0)
        column = lax.broadcasted_iota(jnp.int32, values.shape, 1)
        own = jnp.sum(
            jnp.where(row == group * plane + column, values, 0.0), axis=1, keepdims=True
        )
        result = jnp.where((lane >= 0) & (lane < negatives), own, 0.0)
        if count > 2:
            result = result - pick_scores(0, count - 2)
        early[...] = result

    for load in loads[:3]:
        load.wait()
    rows = jnp.concatenate(
        [
            positive[...].reshape(positive_rows, width),
            query[...].reshape(query_rows, width),
        ],
        axis=0,
    )
    front[parity, shard // 2, : positive_rows + query_rows] = encode(rows, transform[...])
    loads[3].wait()
    labels_buf[...] = jnp.zeros_like(labels_buf)
    labels_buf[:share] = first_token(hidden[:, :16])
    labels_buf[share : share + queries] = first_token(query[:, :16])
    labels_buf[share + queries : share + 2 * queries] = first_token(positive[:, :16])
    numbers, marks = ids_ref[...], teacher_ref[...]
    upper = numbers // 256
    level = (marks + 4096) // 64
    for i, values in enumerate((upper, numbers - upper * 256, level - 64, marks + 4096 - level * 64)):
        labels_buf[
            share + 2 * queries : share + 3 * queries, i * negatives : (i + 1) * negatives
        ] = values.astype(jnp.float32)
    front[parity, shard // 2, positive_rows + query_rows :] = labels_buf[...].astype(jnp.bfloat16)
    pl.semaphore_wait(barrier, shards + groups - 2)

    send_own(0)
    for chunk in range(1, count):
        first, size = firsts[chunk - 1], sizes[chunk - 1]
        rows = hidden[first : first + size].reshape(size * lp, width)
        coded[parity, shard // 2, first * lp : (first + size) * lp] = encode(rows, transform[...])
        if chunk < min(2, count - 1):
            send_own(chunk)
    pool_buf[...] = jnp.zeros_like(pool_buf)
    loads[4].wait()
    loads[5].wait()

    def pass_on(chunk):
        for level in range(1, bits - 1):
            relay(chunk, level)
            if level == 1 and chunk + 2 < count - 1:
                send_own(chunk + 2)
            if level == 1 and chunk + 2 == count:
                send_own(count - 1)
        send_core(chunk, 0)

    passed = set()

    def pass_last(chunk):
        if chunk in passed:
            return
        passed.add(chunk)
        relay(chunk, bits - 1)
        send_core(chunk, 1)

    pooled = set()

    def consume(chunk, half):
        if chunk > 0 and (chunk, half) not in pooled:
            pooled.add((chunk, half))
            finish(chunk, half)
            pool_half(chunk, half)

    for step in range(count):
        pass_on(step)
        if step == 2:
            pool_positive()
        if step > 2:
            consume(step - 2, 1)
        if step > 0:
            pass_last(step - 1)
        if step > 1 and step == count - 1:
            consume(step - 1, 1)
        consume(step, 0)
        if step == 1:
            finish(0, 0)
            finish(0, 1)
            cls_all[group] = front[:, :, positive_rows + query_rows :]
            for i in range(1, groups):
                z_copy(i, 0).start()
            pool_query()
        if step > 1 and step == count - 2:
            consume(step - 1, 1)
            z_pass()
            pass_last(step)
            dense_work()
    if count < 4:
        for chunk in range(1, count - 1):
            consume(chunk, 1)
        if count < 3:
            pool_positive()
        z_pass()
        dense_work()
    early_scores()
    pass_last(count - 1)
    consume(count - 1, 1)

    late = early[...] - pick_scores(count - 2, count - 1)
    partial[shard] = jnp.sum(late.reshape(total // 8, 8, spread), axis=0)

    for offset in range(shards - 1, 0, -1):
        pltpu.make_async_remote_copy(
            src_ref=partial.at[shard],
            dst_ref=partial.at[shard],
            send_sem=sum_send.at[0],
            recv_sem=sum_recv.at[0],
            device_id={"shard": peers[offset]},
            device_id_type=MESH_ID,
        ).start()
    for source, sem in ((front, 0), (coded, 1)):
        wait_bytes(source.at[0], tree_send.at[sem])
        wait_bytes(source.at[1, : half_slots - 1], tree_send.at[sem])
    wait_bytes(others(0), z_send.at[0])
    wait_bytes(others(1), z_send.at[1])
    wait_bytes(others(0), z_send.at[2])
    wait_bytes(partial.at[: shards - 1], sum_recv.at[0])
    tables[group] = jnp.sum(partial[...], axis=0)
    for i in range(groups - 1, 0, -1):
        pltpu.make_async_remote_copy(
            src_ref=tables.at[group],
            dst_ref=tables.at[group],
            send_sem=sum_send.at[1],
            recv_sem=sum_recv.at[1],
            device_id={"group": (group + i) % groups},
            device_id_type=MESH_ID,
        ).start()
    wait_bytes(partial.at[: shards - 1], sum_send.at[0])
    wait_bytes(tables.at[: groups - 1], sum_recv.at[1])

    other = dense_margin[...]
    summed = jnp.sum(tables[...], axis=0) * (1.0 / math.sqrt(vocab_total))
    margins = []
    for k in range(negatives):
        column = jnp.concatenate(
            [
                summed[:, j * negatives + k : j * negatives + k + 1]
                for j in range(total // 8)
            ],
            axis=0,
        )
        margins.append(column + other[:, k : k + 1])
    wide = lax.broadcasted_iota(jnp.int32, (total, LANES), 1)
    margin = jnp.zeros((total, LANES), jnp.float32)
    for k in range(negatives):
        margin = jnp.where(wide == k, margins[k], margin)
    margin_buf[...] = margin
    own_row = ((group * 2 + parity) * half_slots + shard // 2) * queries
    margin_out[...] = margin_buf[pl.ds(own_row, queries), :negatives]
    scale = 1.0 / (negatives * math.sqrt(width))
    coefs = [
        (margins[k] - other[:, negatives + k : negatives + k + 1]) * scale
        for k in range(negatives)
    ]
    together = sum(coefs[1:], coefs[0])
    ahead_vec = together * vectors[1]
    ahead_cls = together * states[1]
    for k in range(negatives):
        ahead_vec = ahead_vec - coefs[k] * vectors[2 + k]
        ahead_cls = ahead_cls - coefs[k] * states[2 + k]
    high, low = halves(ahead_vec)
    right_out[:total] = high
    right_out[total : 2 * total] = low
    high, low = halves(ahead_cls)
    left_out[2 * total : 3 * total] = high
    left_out[3 * total : 4 * total] = low
    left_out[4 * total :] = high
    wait_bytes(tables.at[: groups - 1], sum_send.at[1])


def gradient_kernel(
    left, right, margin, margin_out, grad_ref
):
    margin_out[...] = margin[...]
    grad_ref[...] = lax.dot_general(
        left[...],
        right[...],
        (((0,), (0,)), ((), ())),
        preferred_element_type=jnp.float32,
    )


def body(
    query_hidden,
    positive_hidden,
    passage_store,
    negative_ids,
    teacher_margins,
    transform_weight,
    vocab_weight,
    dense_weight,
):
    groups = lax.axis_size("group")
    shards = lax.axis_size("shard")
    devices = groups * shards
    bits = shards.bit_length() - 1
    queries, lq, width = query_hidden.shape
    store_rows, lp, _ = passage_store.shape
    negatives = negative_ids.shape[1]
    columns = vocab_weight.shape[1]
    share = store_rows // groups
    sizes = chunk_sizes(share)
    count = len(sizes) + 1
    cls_rows = share + 3 * queries
    cls_rows += -cls_rows % 16
    total = devices * queries
    plane = shards * queries
    block_rows = shards // 2 * max(sizes)
    block_rows += -block_rows % 8

    spread = total // 8 * negatives
    spread += -spread % LANES

    vmem = pl.BlockSpec(memory_space=pltpu.VMEM)
    hbm = pl.BlockSpec(memory_space=pltpu.HBM)
    dma = pltpu.SemaphoreType.DMA
    bf16, f32 = jnp.bfloat16, jnp.float32
    def keep(array):
        return pltpu.with_memory_space_constraint(array, pltpu.HBM)

    left, right, margin = pl.pallas_call(
        functools.partial(exchange_kernel, groups, shards, columns * shards, sizes),
        out_shape=[
            jax.ShapeDtypeStruct((5 * total, width), bf16),
            jax.ShapeDtypeStruct((5 * total, width), bf16),
            jax.ShapeDtypeStruct((queries, negatives), f32),
        ],
        in_specs=[vmem] * 2 + [hbm] * 6,
        out_specs=[vmem] * 3,
        scratch_shapes=[
            pltpu.VMEM((queries, lq, width), bf16),
            pltpu.VMEM((queries, lp, width), bf16),
            pltpu.VMEM((width, width), bf16),
            pltpu.VMEM((share, lp, width), bf16),
            pltpu.VMEM((width, columns), bf16),
            pltpu.VMEM((width, width), bf16),
            pltpu.VMEM((cls_rows, width), f32),
            pltpu.VMEM((2, shards // 2, queries * (lq + lp) + cls_rows, width), bf16),
            pltpu.VMEM((2, shards // 2, share * lp, width), bf16),
            pltpu.VMEM((groups, 2, shards // 2, cls_rows, width), bf16),
            pltpu.VMEM((groups, 2 * plane, columns), bf16),
            pltpu.VMEM((plane, columns), f32),
            pltpu.VMEM((len(sizes), 2, block_rows, columns), f32),
            pltpu.VMEM((2 + negatives, total, width), f32),
            pltpu.VMEM((2 + negatives, total, width), f32),
            pltpu.VMEM((negatives, total, LANES), jnp.int32),
            pltpu.VMEM((total, spread), f32),
            pltpu.VMEM((total, LANES), f32),
            pltpu.VMEM((shards, 8, spread), f32),
            pltpu.VMEM((groups, 8, spread), f32),
            pltpu.VMEM((total, LANES), f32),
            dma((6,)),
            dma((2,)),
            dma((count, shards // 2 + 1)),
            dma((3,)),
            dma((3,)),
            dma((2,)),
            dma((2,)),
        ],
        compiler_params=pltpu.CompilerParams(
            collective_id=0, has_side_effects=True, vmem_limit_bytes=40 * 1024 * 1024
        ),
        name="exchange",
    )(
        *map(
            keep,
            (
                negative_ids,
                teacher_margins,
                query_hidden,
                positive_hidden,
                transform_weight,
                passage_store,
                vocab_weight,
                dense_weight,
            ),
        )
    )
    return pl.pallas_call(
        gradient_kernel,
        out_shape=[
            jax.ShapeDtypeStruct((queries, negatives), f32),
            jax.ShapeDtypeStruct((width, width), f32),
        ],
        in_specs=[vmem] * 3,
        out_specs=[vmem] * 2,
        compiler_params=pltpu.CompilerParams(vmem_limit_bytes=24 * 1024 * 1024),
        name="gradient",
    )(left, right, margin)


def solution(mesh):
    in_specs = (
        P(("group", "shard"), None, None),
        P(("group", "shard"), None, None),
        P("shard", None, None),
        P(("group", "shard"), None),
        P(("group", "shard"), None),
        P(),
        P(None, "shard"),
        P(),
    )
    out_specs = (P(("group", "shard"), None), P())
    return jax.shard_map(body, mesh=mesh, in_specs=in_specs, out_specs=out_specs, check_vma=False)
```

```python
import functools
import math

import jax
import jax.numpy as jnp
from jax import lax
from jax.experimental import pallas as pl
from jax.experimental.pallas import tpu as pltpu
from jax.sharding import PartitionSpec as P

COLS = 1920
LANES = 128
MESH_ID = pl.DeviceIdType.MESH


def encode(hidden, transform_weight):
    mixed = jnp.dot(hidden, transform_weight, preferred_element_type=jnp.float32)
    active = 0.5 * mixed * (1.0 + lax.erf(mixed * math.sqrt(0.5)))
    centre = jnp.mean(active, axis=-1, keepdims=True)
    shifted = active - centre
    spread = jnp.mean(shifted * shifted, axis=-1, keepdims=True)
    return (shifted * lax.rsqrt(spread + 1e-05)).astype(jnp.bfloat16)


def chunk_sizes(share):
    sizes = []
    while share > 1:
        sizes.append(2)
        share -= 2
    return sizes + [1] * share


def halves(values):
    high = values.astype(jnp.bfloat16)
    return high, (values - high.astype(jnp.float32)).astype(jnp.bfloat16)


def exchange_kernel(
    groups,
    shards,
    vocab_total,
    sizes,
    ids_ref,
    teacher_ref,
    query_hbm,
    positive_hbm,
    transform_hbm,
    store_hbm,
    vocab_hbm,
    dense_hbm,
    left_out,
    right_out,
    margin_out,
    query,
    positive,
    transform,
    hidden,
    vocab,
    dense,
    labels_buf,
    front,
    coded,
    cls_all,
    query_pool,
    positive_pool,
    pool_buf,
    states,
    vectors,
    places,
    early,
    dense_margin,
    partial,
    tables,
    margin_buf,
    load_sem,
    tree_send,
    tree_recv,
    twin_recv,
    z_send,
    z_recv,
    sum_send,
    sum_recv,
):
    group = lax.axis_index("group")
    shard = lax.axis_index("shard")
    devices = groups * shards
    linear = group * shards + shard
    bits = shards.bit_length() - 1
    queries, lq, width = query.shape
    share, lp, _ = hidden.shape
    columns = vocab.shape[1]
    negatives = ids_ref.shape[1]
    store_rows = share * groups
    cls_rows = cls_all.shape[3]
    total = devices * queries
    plane = shards * queries
    half_slots = shards // 2
    quarter = shards // 4
    parity = shard % 2
    top = shard // half_slots
    block_rows = pool_buf.shape[1]
    firsts = [sum(sizes[:c]) for c in range(len(sizes))]
    count = len(sizes) + 1
    last_unit = 2 + (len(sizes) - 1) * quarter
    positive_rows = queries * lp
    query_rows = queries * lq

    digit = [(shard // (1 << i)) % 2 for i in range(bits)]

    def partner(offset):
        index = 0
        for i in range(bits):
            index = index + ((1 - digit[i]) if (offset >> i) & 1 else digit[i]) * (1 << i)
        return index

    peers = [partner(offset) for offset in range(shards)]

    pairs = (
        (transform_hbm, transform),
        (query_hbm, query),
        (positive_hbm, positive),
        (store_hbm.at[pl.ds(group * share, share)], hidden),
        (vocab_hbm, vocab),
        (dense_hbm, dense),
    )
    loads = [
        pltpu.make_async_copy(source, target, load_sem.at[i])
        for i, (source, target) in enumerate(pairs)
    ]
    for load in loads:
        load.start()

    barrier = pltpu.get_barrier_semaphore()
    for offset in range(1, shards):
        pl.semaphore_signal(
            barrier, inc=1, device_id={"shard": peers[offset]}, device_id_type=MESH_ID
        )
    for i in range(1, groups):
        pl.semaphore_signal(
            barrier, inc=1, device_id={"group": (group + i) % groups}, device_id_type=MESH_ID
        )

    def block(chunk, slot, piece):
        if chunk == 0:
            start, rows = 0, front.shape[2]
        else:
            start, rows = firsts[chunk - 1] * lp, sizes[chunk - 1] * lp
        middle = (rows // 2 + 15) // 16 * 16
        if piece == 1:
            start, rows = start, middle
        elif piece == 2:
            start, rows = start + middle, rows - middle
        ref = front if chunk == 0 else coded
        return ref.at[slot % 2, slot // 2, pl.ds(start, rows)]

    def order(piece):
        outer = list(range(1, bits))
        return outer if piece == 1 else outer[::-1]

    def channel(offset):
        return offset // 2 - 1

    def hop(chunk, offset, piece, dim):
        ref = block(chunk, peers[offset], piece)
        return pltpu.make_async_remote_copy(
            src_ref=ref,
            dst_ref=ref,
            send_sem=tree_send.at[min(chunk, 1)],
            recv_sem=tree_recv.at[chunk, channel(offset ^ (1 << dim))],
            device_id={"shard": peers[1 << dim]},
            device_id_type=MESH_ID,
        )

    def send(*key):
        hop(*key).start()

    def send_own(chunk):
        for dim in range(1, bits):
            send(chunk, 0, 0, dim)

    def send_twin(ref, sem, place):
        pltpu.make_async_remote_copy(
            src_ref=ref,
            dst_ref=ref,
            send_sem=tree_send.at[sem],
            recv_sem=place,
            device_id={"shard": peers[1]},
            device_id_type=MESH_ID,
        ).start()

    def send_core(chunk, half):
        place = tree_recv.at[chunk, half_slots - 1 + half]
        slots = pl.ds((top if half == 0 else 1 - top) * quarter, quarter)
        if chunk == 0:
            send_twin(front.at[parity, slots], 0, place)
        elif half == 1:
            rows = pl.ds(firsts[chunk - 1] * lp, sizes[chunk - 1] * lp)
            send_twin(coded.at[parity, slots, rows], 1, place)
        else:
            for offset in range(2, half_slots, 2):
                send_twin(block(chunk, peers[offset], 0), 1, place)

    def whole(chunk, slots):
        if chunk == 0:
            return front.at[0, :slots]
        rows = sizes[chunk - 1] * lp
        return coded.at[0, :slots, pl.ds(firsts[chunk - 1] * lp, rows)]

    def arrived(chunk, place, slots):
        ref = whole(chunk, slots)
        pltpu.make_async_copy(ref, ref, tree_recv.at[chunk, place]).wait()

    def relay(chunk, level):
        for offset in range(2, shards, 2):
            if offset.bit_count() == level:
                arrived(chunk, channel(offset), 1)
                for piece in (1, 2):
                    path = order(piece)
                    last = max(path.index(i) for i in range(1, bits) if (offset >> i) & 1)
                    for dim in path[last + 1 :]:
                        send(chunk, offset, piece, dim)

    def finish(chunk, half):
        near = half == 0 and chunk > 0
        arrived(chunk, half_slots - 1 + half, quarter - 1 if near else quarter)

    def first_token(values):
        values = values.astype(jnp.float32)
        token = lax.broadcasted_iota(jnp.int32, values.shape, 1)
        return jnp.sum(jnp.where(token == 0, values, 0.0), axis=1)

    def pool(rows, length):
        parts = []
        sequences = rows.shape[0] // length
        for start in range(0, columns, COLS):
            stop = min(start + COLS, columns)
            logits = jnp.dot(rows, vocab[:, start:stop], preferred_element_type=jnp.float32)
            best = jnp.max(logits.reshape(sequences, length, stop - start), axis=1)
            parts.append((start, stop, jnp.log1p(jnp.maximum(best, 0.0))))
        return parts

    def pool_query():
        rows = front[:, :, positive_rows : positive_rows + query_rows]
        for start, stop, values in pool(rows.reshape(plane * lq, width), lq):
            high = values.astype(jnp.bfloat16).astype(jnp.float32)
            both = jnp.concatenate([high, values - high], axis=0)
            query_pool[group, :, start:stop] = both.astype(jnp.bfloat16)
        for i in range(1, groups):
            z_copy(i, 1).start()

    def pool_positive():
        rows = front[:, :, :positive_rows].reshape(plane * lp, width)
        for start, stop, values in pool(rows, lp):
            positive_pool[:, start:stop] = values

    def pool_into(unit, rows):
        tall = rows.shape[0] // lp
        for first, last, values in pool(rows, lp):
            pool_buf[unit, :tall, first:last] = values

    def pool_half(chunk, half):
        start, size = firsts[chunk - 1] * lp, sizes[chunk - 1]
        unit = 2 + (chunk - 1) * quarter
        if half == 1:
            rows = coded[:, pl.ds((1 - top) * quarter, quarter), start : start + size * lp]
            pool_into(unit + quarter - 1, rows.reshape(half_slots * size * lp, width))
        else:
            for near in range(1, quarter):
                rows = coded[:, peers[2 * near] // 2, start : start + size * lp]
                pool_into(unit + near - 1, rows.reshape(2 * size * lp, width))

    def z_part(kind, slot):
        return query_pool.at[slot] if kind else cls_all.at[slot, parity]

    def z_copy(i, kind):
        return pltpu.make_async_remote_copy(
            src_ref=z_part(kind, group),
            dst_ref=z_part(kind, group),
            send_sem=z_send.at[kind],
            recv_sem=z_recv.at[kind],
            device_id={"group": (group + i) % groups},
            device_id_type=MESH_ID,
        )

    def others(kind):
        if kind == 1:
            return query_pool.at[: groups - 1]
        return cls_all.at[: groups - 1, 0]

    def wait_bytes(ref, sem):
        pltpu.make_async_copy(ref, ref, sem).wait()

    def z_pass():
        wait_bytes(others(0), z_recv.at[0])
        for i in range(1, groups):
            slot = (group + i) % groups
            pltpu.make_async_remote_copy(
                src_ref=cls_all.at[slot, parity],
                dst_ref=cls_all.at[slot, parity],
                send_sem=z_send.at[2],
                recv_sem=z_recv.at[2],
                device_id={"shard": peers[1]},
                device_id_type=MESH_ID,
            ).start()

    def dense_work():
        wait_bytes(others(0), z_recv.at[2])
        table = cls_all[...].reshape(devices * cls_rows, width)
        spots = devices * cls_rows
        spot = lax.broadcasted_iota(jnp.int32, (total, spots), 1)
        row = lax.broadcasted_iota(jnp.int32, (total, spots), 0)
        base = (row // queries) * cls_rows + share + row % queries

        def pick(wanted, values):
            chosen = jnp.where(spot == wanted, 1.0, 0.0).astype(jnp.bfloat16)
            return jnp.dot(chosen, values, preferred_element_type=jnp.float32)

        labels = pick(base + 2 * queries, table[:, :LANES])
        states[0] = pick(base, table)
        states[1] = pick(base + queries, table)
        lane = lax.broadcasted_iota(jnp.int32, (total, LANES), 1)
        for k in range(negatives):
            number = (labels[:, k : k + 1] * 256.0 + labels[:, negatives + k : negatives + k + 1])
            number = number.astype(jnp.int32)
            owner = number // store_rows
            local = number - owner * store_rows
            part = local // share
            inner = local - part * share
            spot_of = (part * 2 + owner % 2) * half_slots + owner // 2
            states[2 + k] = pick(spot_of * cls_rows + inner, table)
            twin = owner % 2
            pair = owner // 2
            apart = jnp.bitwise_xor(pair, shard // 2)
            place = twin * block_rows + inner
            for c, (size, first) in enumerate(zip(sizes, firsts, strict=True)):
                far = (twin * quarter + pair % quarter) * size
                row_here = jnp.where(apart < quarter, twin * size, far) + inner - first
                unit = 1 + c * quarter + jnp.minimum(apart, quarter)
                there = (apart > 0) & (inner >= first) & (inner < first + size)
                place = jnp.where(there, unit * block_rows + row_here, place)
            place = jnp.where(part == group, place, -1)
            places[k] = jnp.broadcast_to(place, (total, LANES))
        flat = states[...].reshape((2 + negatives) * total, width).astype(jnp.bfloat16)
        vectors[...] = jnp.dot(flat, dense[...], preferred_element_type=jnp.float32).reshape(
            vectors.shape
        )
        inv_root = 1.0 / math.sqrt(width)
        query_vec = vectors[0]
        dense_pos = jnp.sum(query_vec * vectors[1], axis=1, keepdims=True)
        result = jnp.zeros((total, LANES), jnp.float32)
        for k in range(negatives):
            dense_neg = jnp.sum(query_vec * vectors[2 + k], axis=1, keepdims=True)
            target = (
                labels[:, 2 * negatives + k : 2 * negatives + k + 1] * 64.0
                + labels[:, 3 * negatives + k : 3 * negatives + k + 1]
            ) / 1024.0
            result = jnp.where(lane == k, (dense_pos - dense_neg) * inv_root, result)
            result = jnp.where(lane == negatives + k, target, result)
        dense_margin[...] = result
        query_bf = states[0].astype(jnp.bfloat16)
        query_high, query_low = halves(query_vec)
        left_out[:total] = query_bf
        left_out[total : 2 * total] = query_bf
        right_out[2 * total : 3 * total] = query_high
        right_out[3 * total : 4 * total] = query_high
        right_out[4 * total : 5 * total] = query_low

    def score(values):
        high, low = halves(values)
        stacked = query_pool[...].reshape(2 * total, columns)
        dims = (((1,), (1,)), ((), ()))
        both = lax.dot_general(
            stacked, high, dims, preferred_element_type=jnp.float32
        ) + lax.dot_general(stacked, low, dims, preferred_element_type=jnp.float32)
        both = both.reshape(groups, 2, plane, values.shape[0])
        return (both[:, 0] + both[:, 1]).reshape(total, values.shape[0])

    spread = partial.shape[2]
    lane = lax.broadcasted_iota(jnp.int32, (total, spread), 1)
    lane -= (lax.broadcasted_iota(jnp.int32, (total, spread), 0) // 8) * negatives

    def pick_scores(first, last):
        rows = (last - first) * block_rows
        values = score(pool_buf[first:last].reshape(rows, columns))
        column = lax.broadcasted_iota(jnp.int32, values.shape, 1) + first * block_rows
        result = jnp.zeros((total, spread), jnp.float32)
        for k in range(negatives):
            hit = column == places[k, :, :rows]
            taken = jnp.sum(jnp.where(hit, values, 0.0), axis=1, keepdims=True)
            result = jnp.where(lane == k, taken, result)
        return result

    def early_scores():
        wait_bytes(others(1), z_recv.at[1])
        values = score(positive_pool[...])
        row = lax.broadcasted_iota(jnp.int32, values.shape, 0)
        column = lax.broadcasted_iota(jnp.int32, values.shape, 1)
        own = jnp.sum(
            jnp.where(row == group * plane + column, values, 0.0), axis=1, keepdims=True
        )
        result = jnp.where((lane >= 0) & (lane < negatives), own, 0.0)
        early[...] = result - pick_scores(0, last_unit)

    for load in loads[:3]:
        load.wait()
    rows = jnp.concatenate(
        [
            positive[...].reshape(positive_rows, width),
            query[...].reshape(query_rows, width),
        ],
        axis=0,
    )
    front[parity, shard // 2, : positive_rows + query_rows] = encode(rows, transform[...])
    loads[3].wait()
    labels_buf[...] = jnp.zeros_like(labels_buf)
    labels_buf[:share] = first_token(hidden[:, :16])
    labels_buf[share : share + queries] = first_token(query[:, :16])
    labels_buf[share + queries : share + 2 * queries] = first_token(positive[:, :16])
    numbers, marks = ids_ref[...], teacher_ref[...]
    upper = numbers // 256
    level = (marks + 4096) // 64
    for i, values in enumerate((upper, numbers - upper * 256, level - 64, marks + 4096 - level * 64)):
        labels_buf[
            share + 2 * queries : share + 3 * queries, i * negatives : (i + 1) * negatives
        ] = values.astype(jnp.float32)
    front[parity, shard // 2, positive_rows + query_rows :] = labels_buf[...].astype(jnp.bfloat16)
    pl.semaphore_wait(barrier, shards + groups - 2)

    send_own(0)
    for chunk in range(1, count):
        first, size = firsts[chunk - 1], sizes[chunk - 1]
        rows = hidden[first : first + size].reshape(size * lp, width)
        coded[parity, shard // 2, first * lp : (first + size) * lp] = encode(rows, transform[...])
        if chunk < min(2, count - 1):
            send_own(chunk)
    send_twin(coded.at[parity, shard // 2], 1, twin_recv.at[0])
    pool_buf[...] = jnp.zeros_like(pool_buf)
    loads[4].wait()
    loads[5].wait()
    pool_into(parity, coded[parity, shard // 2])

    def pass_on(chunk):
        for level in range(1, bits - 1):
            relay(chunk, level)
            if level == 1 and chunk + 2 < count - 1:
                send_own(chunk + 2)
            if level == 1 and chunk + 2 == count:
                send_own(count - 1)
        send_core(chunk, 0)

    passed = set()

    def pass_last(chunk):
        if chunk in passed:
            return
        passed.add(chunk)
        relay(chunk, bits - 1)
        send_core(chunk, 1)

    pooled = set()

    def consume(chunk, half):
        if chunk > 0 and (chunk, half) not in pooled:
            pooled.add((chunk, half))
            finish(chunk, half)
            pool_half(chunk, half)

    for step in range(count):
        pass_on(step)
        if step == 0:
            wait_bytes(coded.at[0, 0], twin_recv.at[0])
            pool_into(1 - parity, coded[1 - parity, shard // 2])
        if step == 2:
            pool_positive()
        if step > 2:
            consume(step - 2, 1)
        if step > 0:
            pass_last(step - 1)
        if step > 1 and step == count - 1:
            consume(step - 1, 1)
        consume(step, 0)
        if step == 1:
            finish(0, 0)
            finish(0, 1)
            cls_all[group] = front[:, :, positive_rows + query_rows :]
            for i in range(1, groups):
                z_copy(i, 0).start()
            pool_query()
        if step > 1 and step == count - 2:
            consume(step - 1, 1)
            z_pass()
            pass_last(step)
            dense_work()
    if count < 4:
        for chunk in range(1, count - 1):
            consume(chunk, 1)
        if count < 3:
            pool_positive()
        z_pass()
        dense_work()
    early_scores()
    pass_last(count - 1)
    consume(count - 1, 1)

    late = early[...] - pick_scores(last_unit, last_unit + quarter)
    partial[shard] = jnp.sum(late.reshape(total // 8, 8, spread), axis=0)

    for offset in range(shards - 1, 0, -1):
        pltpu.make_async_remote_copy(
            src_ref=partial.at[shard],
            dst_ref=partial.at[shard],
            send_sem=sum_send.at[0],
            recv_sem=sum_recv.at[0],
            device_id={"shard": peers[offset]},
            device_id_type=MESH_ID,
        ).start()
    for source, sem in ((front, 0), (coded, 1)):
        wait_bytes(source.at[0], tree_send.at[sem])
        wait_bytes(source.at[1, : half_slots - 1], tree_send.at[sem])
    wait_bytes(others(0), z_send.at[0])
    wait_bytes(others(1), z_send.at[1])
    wait_bytes(others(0), z_send.at[2])
    wait_bytes(partial.at[: shards - 1], sum_recv.at[0])
    tables[group] = jnp.sum(partial[...], axis=0)
    for i in range(groups - 1, 0, -1):
        pltpu.make_async_remote_copy(
            src_ref=tables.at[group],
            dst_ref=tables.at[group],
            send_sem=sum_send.at[1],
            recv_sem=sum_recv.at[1],
            device_id={"group": (group + i) % groups},
            device_id_type=MESH_ID,
        ).start()
    wait_bytes(partial.at[: shards - 1], sum_send.at[0])
    wait_bytes(tables.at[: groups - 1], sum_recv.at[1])

    other = dense_margin[...]
    summed = jnp.sum(tables[...], axis=0) * (1.0 / math.sqrt(vocab_total))
    margins = []
    for k in range(negatives):
        column = jnp.concatenate(
            [
                summed[:, j * negatives + k : j * negatives + k + 1]
                for j in range(total // 8)
            ],
            axis=0,
        )
        margins.append(column + other[:, k : k + 1])
    wide = lax.broadcasted_iota(jnp.int32, (total, LANES), 1)
    margin = jnp.zeros((total, LANES), jnp.float32)
    for k in range(negatives):
        margin = jnp.where(wide == k, margins[k], margin)
    margin_buf[...] = margin
    own_row = ((group * 2 + parity) * half_slots + shard // 2) * queries
    margin_out[...] = margin_buf[pl.ds(own_row, queries), :negatives]
    scale = 1.0 / (negatives * math.sqrt(width))
    coefs = [
        (margins[k] - other[:, negatives + k : negatives + k + 1]) * scale
        for k in range(negatives)
    ]
    together = sum(coefs[1:], coefs[0])
    ahead_vec = together * vectors[1]
    ahead_cls = together * states[1]
    for k in range(negatives):
        ahead_vec = ahead_vec - coefs[k] * vectors[2 + k]
        ahead_cls = ahead_cls - coefs[k] * states[2 + k]
    high, low = halves(ahead_vec)
    right_out[:total] = high
    right_out[total : 2 * total] = low
    high, low = halves(ahead_cls)
    left_out[2 * total : 3 * total] = high
    left_out[3 * total : 4 * total] = low
    left_out[4 * total :] = high
    wait_bytes(tables.at[: groups - 1], sum_send.at[1])


def gradient_kernel(
    left, right, margin, margin_out, grad_ref
):
    margin_out[...] = margin[...]
    grad_ref[...] = lax.dot_general(
        left[...],
        right[...],
        (((0,), (0,)), ((), ())),
        preferred_element_type=jnp.float32,
    )


def body(
    query_hidden,
    positive_hidden,
    passage_store,
    negative_ids,
    teacher_margins,
    transform_weight,
    vocab_weight,
    dense_weight,
):
    groups = lax.axis_size("group")
    shards = lax.axis_size("shard")
    devices = groups * shards
    bits = shards.bit_length() - 1
    queries, lq, width = query_hidden.shape
    store_rows, lp, _ = passage_store.shape
    negatives = negative_ids.shape[1]
    columns = vocab_weight.shape[1]
    share = store_rows // groups
    sizes = chunk_sizes(share)
    count = len(sizes) + 1
    cls_rows = share + 3 * queries
    cls_rows += -cls_rows % 16
    total = devices * queries
    plane = shards * queries
    block_rows = max(shards // 2 * max(sizes), share)
    block_rows += -block_rows % 8

    spread = total // 8 * negatives
    spread += -spread % LANES

    vmem = pl.BlockSpec(memory_space=pltpu.VMEM)
    hbm = pl.BlockSpec(memory_space=pltpu.HBM)
    dma = pltpu.SemaphoreType.DMA
    bf16, f32 = jnp.bfloat16, jnp.float32
    def keep(array):
        return pltpu.with_memory_space_constraint(array, pltpu.HBM)

    left, right, margin = pl.pallas_call(
        functools.partial(exchange_kernel, groups, shards, columns * shards, sizes),
        out_shape=[
            jax.ShapeDtypeStruct((5 * total, width), bf16),
            jax.ShapeDtypeStruct((5 * total, width), bf16),
            jax.ShapeDtypeStruct((queries, negatives), f32),
        ],
        in_specs=[vmem] * 2 + [hbm] * 6,
        out_specs=[vmem] * 3,
        scratch_shapes=[
            pltpu.VMEM((queries, lq, width), bf16),
            pltpu.VMEM((queries, lp, width), bf16),
            pltpu.VMEM((width, width), bf16),
            pltpu.VMEM((share, lp, width), bf16),
            pltpu.VMEM((width, columns), bf16),
            pltpu.VMEM((width, width), bf16),
            pltpu.VMEM((cls_rows, width), f32),
            pltpu.VMEM((2, shards // 2, queries * (lq + lp) + cls_rows, width), bf16),
            pltpu.VMEM((2, shards // 2, share * lp, width), bf16),
            pltpu.VMEM((groups, 2, shards // 2, cls_rows, width), bf16),
            pltpu.VMEM((groups, 2 * plane, columns), bf16),
            pltpu.VMEM((plane, columns), f32),
            pltpu.VMEM((2 + len(sizes) * (shards // 4), block_rows, columns), f32),
            pltpu.VMEM((2 + negatives, total, width), f32),
            pltpu.VMEM((2 + negatives, total, width), f32),
            pltpu.VMEM((negatives, total, LANES), jnp.int32),
            pltpu.VMEM((total, spread), f32),
            pltpu.VMEM((total, LANES), f32),
            pltpu.VMEM((shards, 8, spread), f32),
            pltpu.VMEM((groups, 8, spread), f32),
            pltpu.VMEM((total, LANES), f32),
            dma((6,)),
            dma((2,)),
            dma((count, shards // 2 + 1)),
            dma((1,)),
            dma((3,)),
            dma((3,)),
            dma((2,)),
            dma((2,)),
        ],
        compiler_params=pltpu.CompilerParams(
            collective_id=0, has_side_effects=True, vmem_limit_bytes=40 * 1024 * 1024
        ),
        name="exchange",
    )(
        *map(
            keep,
            (
                negative_ids,
                teacher_margins,
                query_hidden,
                positive_hidden,
                transform_weight,
                passage_store,
                vocab_weight,
                dense_weight,
            ),
        )
    )
    return pl.pallas_call(
        gradient_kernel,
        out_shape=[
            jax.ShapeDtypeStruct((queries, negatives), f32),
            jax.ShapeDtypeStruct((width, width), f32),
        ],
        in_specs=[vmem] * 3,
        out_specs=[vmem] * 2,
        compiler_params=pltpu.CompilerParams(vmem_limit_bytes=24 * 1024 * 1024),
        name="gradient",
    )(left, right, margin)


def solution(mesh):
    in_specs = (
        P(("group", "shard"), None, None),
        P(("group", "shard"), None, None),
        P("shard", None, None),
        P(("group", "shard"), None),
        P(("group", "shard"), None),
        P(),
        P(None, "shard"),
        P(),
    )
    out_specs = (P(("group", "shard"), None), P())
    return jax.shard_map(body, mesh=mesh, in_specs=in_specs, out_specs=out_specs, check_vma=False)
```

```python
import functools
import math

import jax
import jax.numpy as jnp
from jax import lax
from jax.experimental import pallas as pl
from jax.experimental.pallas import tpu as pltpu
from jax.sharding import PartitionSpec as P

COLS = 1920
LANES = 128
MESH_ID = pl.DeviceIdType.MESH


def encode(hidden, transform_weight):
    mixed = jnp.dot(hidden, transform_weight, preferred_element_type=jnp.float32)
    active = 0.5 * mixed * (1.0 + lax.erf(mixed * math.sqrt(0.5)))
    centre = jnp.mean(active, axis=-1, keepdims=True)
    shifted = active - centre
    spread = jnp.mean(shifted * shifted, axis=-1, keepdims=True)
    return (shifted * lax.rsqrt(spread + 1e-05)).astype(jnp.bfloat16)


def chunk_sizes(share):
    sizes = []
    while share > 1:
        sizes.append(2)
        share -= 2
    return sizes + [1] * share


def halves(values):
    high = values.astype(jnp.bfloat16)
    return high, (values - high.astype(jnp.float32)).astype(jnp.bfloat16)


def exchange_kernel(
    groups,
    shards,
    vocab_total,
    sizes,
    ids_ref,
    teacher_ref,
    query_hbm,
    positive_hbm,
    transform_hbm,
    store_hbm,
    vocab_hbm,
    dense_hbm,
    left_out,
    right_out,
    margin_out,
    query,
    positive,
    transform,
    hidden,
    vocab,
    dense,
    labels_buf,
    front,
    coded,
    cls_all,
    query_pool,
    positive_pool,
    pool_buf,
    states,
    vectors,
    places,
    early,
    dense_margin,
    partial,
    tables,
    margin_buf,
    load_sem,
    tree_send,
    tree_recv,
    twin_recv,
    z_send,
    z_recv,
    sum_send,
    sum_recv,
):
    group = lax.axis_index("group")
    shard = lax.axis_index("shard")
    devices = groups * shards
    linear = group * shards + shard
    bits = shards.bit_length() - 1
    queries, lq, width = query.shape
    share, lp, _ = hidden.shape
    columns = vocab.shape[1]
    negatives = ids_ref.shape[1]
    store_rows = share * groups
    cls_rows = cls_all.shape[3]
    total = devices * queries
    plane = shards * queries
    half_slots = shards // 2
    quarter = shards // 4
    parity = shard % 2
    top = shard // half_slots
    block_rows = pool_buf.shape[1]
    firsts = [sum(sizes[:c]) for c in range(len(sizes))]
    count = len(sizes) + 1
    last_unit = 2 + (len(sizes) - 1) * quarter
    positive_rows = queries * lp
    query_rows = queries * lq

    digit = [(shard // (1 << i)) % 2 for i in range(bits)]

    def partner(offset):
        index = 0
        for i in range(bits):
            index = index + ((1 - digit[i]) if (offset >> i) & 1 else digit[i]) * (1 << i)
        return index

    peers = [partner(offset) for offset in range(shards)]

    pairs = (
        (transform_hbm, transform),
        (query_hbm, query),
        (positive_hbm, positive),
        (store_hbm.at[pl.ds(group * share, share)], hidden),
        (vocab_hbm, vocab),
        (dense_hbm, dense),
    )
    loads = [
        pltpu.make_async_copy(source, target, load_sem.at[i])
        for i, (source, target) in enumerate(pairs)
    ]
    for load in loads:
        load.start()

    barrier = pltpu.get_barrier_semaphore()
    for offset in range(1, shards):
        pl.semaphore_signal(
            barrier, inc=1, device_id={"shard": peers[offset]}, device_id_type=MESH_ID
        )
    for i in range(1, groups):
        pl.semaphore_signal(
            barrier, inc=1, device_id={"group": (group + i) % groups}, device_id_type=MESH_ID
        )

    def block(chunk, slot, piece):
        if chunk == 0:
            start, rows = 0, front.shape[2]
        else:
            start, rows = firsts[chunk - 1] * lp, sizes[chunk - 1] * lp
        middle = (rows // 2 + 15) // 16 * 16
        if piece == 1:
            start, rows = start, middle
        elif piece == 2:
            start, rows = start + middle, rows - middle
        ref = front if chunk == 0 else coded
        return ref.at[slot % 2, slot // 2, pl.ds(start, rows)]

    def order(piece):
        outer = list(range(1, bits))
        return outer if piece == 1 else outer[::-1]

    def channel(offset):
        return offset // 2 - 1

    def hop(chunk, offset, piece, dim):
        ref = block(chunk, peers[offset], piece)
        return pltpu.make_async_remote_copy(
            src_ref=ref,
            dst_ref=ref,
            send_sem=tree_send.at[min(chunk, 1)],
            recv_sem=tree_recv.at[chunk, channel(offset ^ (1 << dim))],
            device_id={"shard": peers[1 << dim]},
            device_id_type=MESH_ID,
        )

    def send(*key):
        hop(*key).start()

    def send_own(chunk):
        for dim in range(1, bits):
            send(chunk, 0, 0, dim)

    def send_twin(ref, sem, place):
        pltpu.make_async_remote_copy(
            src_ref=ref,
            dst_ref=ref,
            send_sem=tree_send.at[sem],
            recv_sem=place,
            device_id={"shard": peers[1]},
            device_id_type=MESH_ID,
        ).start()

    def send_core(chunk, half):
        place = tree_recv.at[chunk, half_slots - 1 + half]
        slots = pl.ds((top if half == 0 else 1 - top) * quarter, quarter)
        if chunk == 0:
            send_twin(front.at[parity, slots], 0, place)
        elif half == 1:
            rows = pl.ds(firsts[chunk - 1] * lp, sizes[chunk - 1] * lp)
            send_twin(coded.at[parity, slots, rows], 1, place)
        else:
            for offset in range(2, half_slots, 2):
                send_twin(block(chunk, peers[offset], 0), 1, place)

    def whole(chunk, slots):
        if chunk == 0:
            return front.at[0, :slots]
        rows = sizes[chunk - 1] * lp
        return coded.at[0, :slots, pl.ds(firsts[chunk - 1] * lp, rows)]

    def arrived(chunk, place, slots):
        ref = whole(chunk, slots)
        pltpu.make_async_copy(ref, ref, tree_recv.at[chunk, place]).wait()

    def relay(chunk, level):
        for offset in range(2, shards, 2):
            if offset.bit_count() == level:
                arrived(chunk, channel(offset), 1)
                for piece in (1, 2):
                    path = order(piece)
                    last = max(path.index(i) for i in range(1, bits) if (offset >> i) & 1)
                    for dim in path[last + 1 :]:
                        send(chunk, offset, piece, dim)

    def finish(chunk, half):
        near = half == 0 and chunk > 0
        arrived(chunk, half_slots - 1 + half, quarter - 1 if near else quarter)

    def first_token(values):
        values = values.astype(jnp.float32)
        token = lax.broadcasted_iota(jnp.int32, values.shape, 1)
        return jnp.sum(jnp.where(token == 0, values, 0.0), axis=1)

    def pool(rows, length):
        parts = []
        sequences = rows.shape[0] // length
        for start in range(0, columns, COLS):
            stop = min(start + COLS, columns)
            logits = jnp.dot(rows, vocab[:, start:stop], preferred_element_type=jnp.float32)
            best = jnp.max(logits.reshape(sequences, length, stop - start), axis=1)
            parts.append((start, stop, jnp.log1p(jnp.maximum(best, 0.0))))
        return parts

    def pool_query():
        rows = front[:, :, positive_rows : positive_rows + query_rows]
        for start, stop, values in pool(rows.reshape(plane * lq, width), lq):
            high = values.astype(jnp.bfloat16).astype(jnp.float32)
            both = jnp.concatenate([high, values - high], axis=0)
            query_pool[group, :, start:stop] = both.astype(jnp.bfloat16)
        for i in range(1, groups):
            z_copy(i, 1).start()

    def pool_positive():
        rows = front[:, :, :positive_rows].reshape(plane * lp, width)
        for start, stop, values in pool(rows, lp):
            positive_pool[:, start:stop] = values

    def pool_into(unit, rows):
        tall = rows.shape[0] // lp
        for first, last, values in pool(rows, lp):
            pool_buf[unit, :tall, first:last] = values

    def pool_half(chunk, half):
        start, size = firsts[chunk - 1] * lp, sizes[chunk - 1]
        unit = 2 + (chunk - 1) * quarter
        if half == 1:
            rows = coded[:, pl.ds((1 - top) * quarter, quarter), start : start + size * lp]
            pool_into(unit + quarter - 1, rows.reshape(half_slots * size * lp, width))
        else:
            for near in range(1, quarter):
                rows = coded[:, peers[2 * near] // 2, start : start + size * lp]
                pool_into(unit + near - 1, rows.reshape(2 * size * lp, width))

    def z_part(kind, slot):
        return query_pool.at[slot] if kind else cls_all.at[slot, parity]

    def z_copy(i, kind):
        return pltpu.make_async_remote_copy(
            src_ref=z_part(kind, group),
            dst_ref=z_part(kind, group),
            send_sem=z_send.at[kind],
            recv_sem=z_recv.at[kind],
            device_id={"group": (group + i) % groups},
            device_id_type=MESH_ID,
        )

    def others(kind):
        if kind == 1:
            return query_pool.at[: groups - 1]
        return cls_all.at[: groups - 1, 0]

    def wait_bytes(ref, sem):
        pltpu.make_async_copy(ref, ref, sem).wait()

    def z_pass():
        wait_bytes(others(0), z_recv.at[0])
        for i in range(1, groups):
            slot = (group + i) % groups
            pltpu.make_async_remote_copy(
                src_ref=cls_all.at[slot, parity],
                dst_ref=cls_all.at[slot, parity],
                send_sem=z_send.at[2],
                recv_sem=z_recv.at[2],
                device_id={"shard": peers[1]},
                device_id_type=MESH_ID,
            ).start()

    def dense_work():
        wait_bytes(others(0), z_recv.at[2])
        table = cls_all[...].reshape(devices * cls_rows, width)
        spots = devices * cls_rows
        spot = lax.broadcasted_iota(jnp.int32, (total, spots), 1)
        row = lax.broadcasted_iota(jnp.int32, (total, spots), 0)
        base = (row // queries) * cls_rows + share + row % queries

        def pick(wanted, values):
            chosen = jnp.where(spot == wanted, 1.0, 0.0).astype(jnp.bfloat16)
            return jnp.dot(chosen, values, preferred_element_type=jnp.float32)

        labels = pick(base + 2 * queries, table[:, :LANES])
        states[0] = pick(base, table)
        states[1] = pick(base + queries, table)
        lane = lax.broadcasted_iota(jnp.int32, (total, LANES), 1)
        for k in range(negatives):
            number = (labels[:, k : k + 1] * 256.0 + labels[:, negatives + k : negatives + k + 1])
            number = number.astype(jnp.int32)
            owner = number // store_rows
            local = number - owner * store_rows
            part = local // share
            inner = local - part * share
            spot_of = (part * 2 + owner % 2) * half_slots + owner // 2
            states[2 + k] = pick(spot_of * cls_rows + inner, table)
            twin = owner % 2
            pair = owner // 2
            apart = jnp.bitwise_xor(pair, shard // 2)
            place = twin * block_rows + inner
            for c, (size, first) in enumerate(zip(sizes, firsts, strict=True)):
                far = (twin * quarter + pair % quarter) * size
                row_here = jnp.where(apart < quarter, twin * size, far) + inner - first
                unit = 1 + c * quarter + jnp.minimum(apart, quarter)
                there = (apart > 0) & (inner >= first) & (inner < first + size)
                place = jnp.where(there, unit * block_rows + row_here, place)
            place = jnp.where(part == group, place, -1)
            places[k] = jnp.broadcast_to(place, (total, LANES))
        flat = states[...].reshape((2 + negatives) * total, width).astype(jnp.bfloat16)
        vectors[...] = jnp.dot(flat, dense[...], preferred_element_type=jnp.float32).reshape(
            vectors.shape
        )
        inv_root = 1.0 / math.sqrt(width)
        query_vec = vectors[0]
        dense_pos = jnp.sum(query_vec * vectors[1], axis=1, keepdims=True)
        result = jnp.zeros((total, LANES), jnp.float32)
        for k in range(negatives):
            dense_neg = jnp.sum(query_vec * vectors[2 + k], axis=1, keepdims=True)
            target = (
                labels[:, 2 * negatives + k : 2 * negatives + k + 1] * 64.0
                + labels[:, 3 * negatives + k : 3 * negatives + k + 1]
            ) / 1024.0
            result = jnp.where(lane == k, (dense_pos - dense_neg) * inv_root, result)
            result = jnp.where(lane == negatives + k, target, result)
        dense_margin[...] = result
        query_bf = states[0].astype(jnp.bfloat16)
        query_high, query_low = halves(query_vec)
        left_out[:total] = query_bf
        left_out[total : 2 * total] = query_bf
        right_out[2 * total : 3 * total] = query_high
        right_out[3 * total : 4 * total] = query_high
        right_out[4 * total : 5 * total] = query_low

    def score(values):
        high, low = halves(values)
        stacked = query_pool[...].reshape(2 * total, columns)
        dims = (((1,), (1,)), ((), ()))
        both = lax.dot_general(
            stacked, high, dims, preferred_element_type=jnp.float32
        ) + lax.dot_general(stacked, low, dims, preferred_element_type=jnp.float32)
        both = both.reshape(groups, 2, plane, values.shape[0])
        return (both[:, 0] + both[:, 1]).reshape(total, values.shape[0])

    spread = partial.shape[2]
    lane = lax.broadcasted_iota(jnp.int32, (total, spread), 1)
    lane -= (lax.broadcasted_iota(jnp.int32, (total, spread), 0) // 8) * negatives

    def pick_scores(first, last):
        rows = (last - first) * block_rows
        values = score(pool_buf[first:last].reshape(rows, columns))
        column = lax.broadcasted_iota(jnp.int32, values.shape, 1) + first * block_rows
        result = jnp.zeros((total, spread), jnp.float32)
        for k in range(negatives):
            hit = column == places[k, :, :rows]
            taken = jnp.sum(jnp.where(hit, values, 0.0), axis=1, keepdims=True)
            result = jnp.where(lane == k, taken, result)
        return result

    def early_scores():
        wait_bytes(others(1), z_recv.at[1])
        values = score(positive_pool[...])
        row = lax.broadcasted_iota(jnp.int32, values.shape, 0)
        column = lax.broadcasted_iota(jnp.int32, values.shape, 1)
        own = jnp.sum(
            jnp.where(row == group * plane + column, values, 0.0), axis=1, keepdims=True
        )
        result = jnp.where((lane >= 0) & (lane < negatives), own, 0.0)
        early[...] = result - pick_scores(0, last_unit)

    for load in loads[:3]:
        load.wait()
    rows = jnp.concatenate(
        [
            positive[...].reshape(positive_rows, width),
            query[...].reshape(query_rows, width),
        ],
        axis=0,
    )
    front[parity, shard // 2, : positive_rows + query_rows] = encode(rows, transform[...])
    loads[3].wait()
    labels_buf[...] = jnp.zeros_like(labels_buf)
    labels_buf[:share] = first_token(hidden[:, :16])
    labels_buf[share : share + queries] = first_token(query[:, :16])
    labels_buf[share + queries : share + 2 * queries] = first_token(positive[:, :16])
    numbers, marks = ids_ref[...], teacher_ref[...]
    upper = numbers // 256
    level = (marks + 4096) // 64
    for i, values in enumerate((upper, numbers - upper * 256, level - 64, marks + 4096 - level * 64)):
        labels_buf[
            share + 2 * queries : share + 3 * queries, i * negatives : (i + 1) * negatives
        ] = values.astype(jnp.float32)
    front[parity, shard // 2, positive_rows + query_rows :] = labels_buf[...].astype(jnp.bfloat16)
    pl.semaphore_wait(barrier, shards + groups - 2)

    send_own(0)
    for chunk in range(1, count):
        first, size = firsts[chunk - 1], sizes[chunk - 1]
        rows = hidden[first : first + size].reshape(size * lp, width)
        coded[parity, shard // 2, first * lp : (first + size) * lp] = encode(rows, transform[...])
        if chunk < min(2, count - 1):
            send_own(chunk)
    send_twin(coded.at[parity, shard // 2], 1, twin_recv.at[0])
    pool_buf[...] = jnp.zeros_like(pool_buf)
    loads[4].wait()
    loads[5].wait()
    pool_into(parity, coded[parity, shard // 2])

    def pass_on(chunk):
        for level in range(1, bits - 1):
            relay(chunk, level)
            if level == 1 and chunk + 2 < count - 1:
                send_own(chunk + 2)
            if level == 1 and chunk + 2 == count:
                send_own(count - 1)
        send_core(chunk, 0)

    passed = set()

    def pass_last(chunk):
        if chunk in passed:
            return
        passed.add(chunk)
        relay(chunk, bits - 1)
        send_core(chunk, 1)

    pooled = set()

    def consume(chunk, half):
        if chunk > 0 and (chunk, half) not in pooled:
            pooled.add((chunk, half))
            finish(chunk, half)
            pool_half(chunk, half)

    for step in range(count):
        pass_on(step)
        if step == 0:
            wait_bytes(coded.at[0, 0], twin_recv.at[0])
            pool_into(1 - parity, coded[1 - parity, shard // 2])
        if step == 2:
            pool_positive()
        if step > 2:
            consume(step - 2, 1)
        if step > 0:
            pass_last(step - 1)
        if step > 1 and step == count - 1:
            consume(step - 1, 1)
        consume(step, 0)
        if step == 1:
            finish(0, 0)
            finish(0, 1)
            cls_all[group] = front[:, :, positive_rows + query_rows :]
            for i in range(1, groups):
                z_copy(i, 0).start()
            pool_query()
        if step == 2 and step < count - 2:
            consume(step - 1, 1)
        if step > 1 and step == count - 2:
            consume(step - 1, 1)
            z_pass()
            pass_last(step)
            dense_work()
    if count < 4:
        for chunk in range(1, count - 1):
            consume(chunk, 1)
        if count < 3:
            pool_positive()
        z_pass()
        dense_work()
    early_scores()
    pass_last(count - 1)
    consume(count - 1, 1)

    late = early[...] - pick_scores(last_unit, last_unit + quarter)
    partial[shard] = jnp.sum(late.reshape(total // 8, 8, spread), axis=0)

    for offset in range(shards - 1, 0, -1):
        pltpu.make_async_remote_copy(
            src_ref=partial.at[shard],
            dst_ref=partial.at[shard],
            send_sem=sum_send.at[0],
            recv_sem=sum_recv.at[0],
            device_id={"shard": peers[offset]},
            device_id_type=MESH_ID,
        ).start()
    for source, sem in ((front, 0), (coded, 1)):
        wait_bytes(source.at[0], tree_send.at[sem])
        wait_bytes(source.at[1, : half_slots - 1], tree_send.at[sem])
    wait_bytes(others(0), z_send.at[0])
    wait_bytes(others(1), z_send.at[1])
    wait_bytes(others(0), z_send.at[2])
    wait_bytes(partial.at[: shards - 1], sum_recv.at[0])
    tables[group] = jnp.sum(partial[...], axis=0)
    for i in range(groups - 1, 0, -1):
        pltpu.make_async_remote_copy(
            src_ref=tables.at[group],
            dst_ref=tables.at[group],
            send_sem=sum_send.at[1],
            recv_sem=sum_recv.at[1],
            device_id={"group": (group + i) % groups},
            device_id_type=MESH_ID,
        ).start()
    wait_bytes(partial.at[: shards - 1], sum_send.at[0])
    wait_bytes(tables.at[: groups - 1], sum_recv.at[1])

    other = dense_margin[...]
    summed = jnp.sum(tables[...], axis=0) * (1.0 / math.sqrt(vocab_total))
    margins = []
    for k in range(negatives):
        column = jnp.concatenate(
            [
                summed[:, j * negatives + k : j * negatives + k + 1]
                for j in range(total // 8)
            ],
            axis=0,
        )
        margins.append(column + other[:, k : k + 1])
    wide = lax.broadcasted_iota(jnp.int32, (total, LANES), 1)
    margin = jnp.zeros((total, LANES), jnp.float32)
    for k in range(negatives):
        margin = jnp.where(wide == k, margins[k], margin)
    margin_buf[...] = margin
    own_row = ((group * 2 + parity) * half_slots + shard // 2) * queries
    margin_out[...] = margin_buf[pl.ds(own_row, queries), :negatives]
    scale = 1.0 / (negatives * math.sqrt(width))
    coefs = [
        (margins[k] - other[:, negatives + k : negatives + k + 1]) * scale
        for k in range(negatives)
    ]
    together = sum(coefs[1:], coefs[0])
    ahead_vec = together * vectors[1]
    ahead_cls = together * states[1]
    for k in range(negatives):
        ahead_vec = ahead_vec - coefs[k] * vectors[2 + k]
        ahead_cls = ahead_cls - coefs[k] * states[2 + k]
    high, low = halves(ahead_vec)
    right_out[:total] = high
    right_out[total : 2 * total] = low
    high, low = halves(ahead_cls)
    left_out[2 * total : 3 * total] = high
    left_out[3 * total : 4 * total] = low
    left_out[4 * total :] = high
    wait_bytes(tables.at[: groups - 1], sum_send.at[1])


def gradient_kernel(
    left, right, margin, margin_out, grad_ref
):
    margin_out[...] = margin[...]
    grad_ref[...] = lax.dot_general(
        left[...],
        right[...],
        (((0,), (0,)), ((), ())),
        preferred_element_type=jnp.float32,
    )


def body(
    query_hidden,
    positive_hidden,
    passage_store,
    negative_ids,
    teacher_margins,
    transform_weight,
    vocab_weight,
    dense_weight,
):
    groups = lax.axis_size("group")
    shards = lax.axis_size("shard")
    devices = groups * shards
    bits = shards.bit_length() - 1
    queries, lq, width = query_hidden.shape
    store_rows, lp, _ = passage_store.shape
    negatives = negative_ids.shape[1]
    columns = vocab_weight.shape[1]
    share = store_rows // groups
    sizes = chunk_sizes(share)
    count = len(sizes) + 1
    cls_rows = share + 3 * queries
    cls_rows += -cls_rows % 16
    total = devices * queries
    plane = shards * queries
    block_rows = max(shards // 2 * max(sizes), share)
    block_rows += -block_rows % 8

    spread = total // 8 * negatives
    spread += -spread % LANES

    vmem = pl.BlockSpec(memory_space=pltpu.VMEM)
    hbm = pl.BlockSpec(memory_space=pltpu.HBM)
    dma = pltpu.SemaphoreType.DMA
    bf16, f32 = jnp.bfloat16, jnp.float32
    def keep(array):
        return pltpu.with_memory_space_constraint(array, pltpu.HBM)

    left, right, margin = pl.pallas_call(
        functools.partial(exchange_kernel, groups, shards, columns * shards, sizes),
        out_shape=[
            jax.ShapeDtypeStruct((5 * total, width), bf16),
            jax.ShapeDtypeStruct((5 * total, width), bf16),
            jax.ShapeDtypeStruct((queries, negatives), f32),
        ],
        in_specs=[vmem] * 2 + [hbm] * 6,
        out_specs=[vmem] * 3,
        scratch_shapes=[
            pltpu.VMEM((queries, lq, width), bf16),
            pltpu.VMEM((queries, lp, width), bf16),
            pltpu.VMEM((width, width), bf16),
            pltpu.VMEM((share, lp, width), bf16),
            pltpu.VMEM((width, columns), bf16),
            pltpu.VMEM((width, width), bf16),
            pltpu.VMEM((cls_rows, width), f32),
            pltpu.VMEM((2, shards // 2, queries * (lq + lp) + cls_rows, width), bf16),
            pltpu.VMEM((2, shards // 2, share * lp, width), bf16),
            pltpu.VMEM((groups, 2, shards // 2, cls_rows, width), bf16),
            pltpu.VMEM((groups, 2 * plane, columns), bf16),
            pltpu.VMEM((plane, columns), f32),
            pltpu.VMEM((2 + len(sizes) * (shards // 4), block_rows, columns), f32),
            pltpu.VMEM((2 + negatives, total, width), f32),
            pltpu.VMEM((2 + negatives, total, width), f32),
            pltpu.VMEM((negatives, total, LANES), jnp.int32),
            pltpu.VMEM((total, spread), f32),
            pltpu.VMEM((total, LANES), f32),
            pltpu.VMEM((shards, 8, spread), f32),
            pltpu.VMEM((groups, 8, spread), f32),
            pltpu.VMEM((total, LANES), f32),
            dma((6,)),
            dma((2,)),
            dma((count, shards // 2 + 1)),
            dma((1,)),
            dma((3,)),
            dma((3,)),
            dma((2,)),
            dma((2,)),
        ],
        compiler_params=pltpu.CompilerParams(
            collective_id=0, has_side_effects=True, vmem_limit_bytes=40 * 1024 * 1024
        ),
        name="exchange",
    )(
        *map(
            keep,
            (
                negative_ids,
                teacher_margins,
                query_hidden,
                positive_hidden,
                transform_weight,
                passage_store,
                vocab_weight,
                dense_weight,
            ),
        )
    )
    return pl.pallas_call(
        gradient_kernel,
        out_shape=[
            jax.ShapeDtypeStruct((queries, negatives), f32),
            jax.ShapeDtypeStruct((width, width), f32),
        ],
        in_specs=[vmem] * 3,
        out_specs=[vmem] * 2,
        compiler_params=pltpu.CompilerParams(vmem_limit_bytes=24 * 1024 * 1024),
        name="gradient",
    )(left, right, margin)


def solution(mesh):
    in_specs = (
        P(("group", "shard"), None, None),
        P(("group", "shard"), None, None),
        P("shard", None, None),
        P(("group", "shard"), None),
        P(("group", "shard"), None),
        P(),
        P(None, "shard"),
        P(),
    )
    out_specs = (P(("group", "shard"), None), P())
    return jax.shard_map(body, mesh=mesh, in_specs=in_specs, out_specs=out_specs, check_vma=False)
```
